512 devices in a mesh: sector: 64 (over z, y_lo, core), radial: 8 (over x, y_hi).
Axes of the slice: x: 4, y: 4 (y_hi: 2, y_lo: 2; y = y_hi * 2 + y_lo), z: 16, core: 2. Of those that a mesh axis runs over, the one named last changes fastest.
Arguments:
- fields: float32 [64, 8, 140, 1024], P('sector', 'radial'), may hold values from -6 to 6
- pattern: int32 [64, 8, 1024], P('sector', 'radial'), may hold values from 0 to 15
- tent_order: int32 [64, 8, 1024], P('sector', 'radial'), may hold values from 0 to 1023, each once within a row
- level_sizes: int32 [64, 8, 4], P('sector', 'radial'), may hold values from 1 to 384, 1024 in all within a row
- send_rows: int32 [64, 8, 4, 128], P('sector', 'radial'), may hold values from 0 to 1023
- neighbours: int32 [64, 8, 4, 1024], P('sector', 'radial'), may hold values from 0 to 1535, as said below
- operator: float32 [140, 140], replicated, may hold values from -2 to 2, as said below
- trace_map: float32 [60, 140], replicated, may hold values from -0.5 to 0.5
- lift_map: float32 [4, 140, 60], replicated, may hold values from -0.375 to 0.375
- tent_height: float32 [16], replicated, may hold values from 0.15 to 0.5
Outputs:
- advanced: float32 [64, 8, 140, 1024], P('sector', 'radial')
The draws below stay inside these ranges and needn't reach their ends.
Inputs may be any that keep to these rules, and one draw needn't show every extreme that they name: `tent_order`: each block's entries are a permutation of 0 to 1023. `level_sizes`: each block's 4 sizes sum to 1024, and some level of every block has exactly 384 tents. `neighbours`: an entry below 1024 names an element of the same block; an entry 1024 + d * 128 + j names the j-th received trace of group d of extended; each of these 512 slots is named by face 0 of exactly one element of the block. `operator`: a skew-symmetric matrix minus a diagonal of positive damping rates.
All inputs are finite; a program needn't handle non-finite values.
Results may differ from the reference program's by a relative error of at most 0.0003.
Values sent between devices are 32-bit elements; how exact they have to be, the bound alone decides.
A program may use at most 64 MiB of HBM per device.

```python
import math
import jax
import jax.numpy as jnp
import numpy as np
from jax import lax

FACES = 4
PATTERNS = 16
LEVELS = 4
SUBSTEPS = 2
TERMS = 4
ELEMS = 1024
COMP = 140
TRACE = 60
BND = 128
BLOCK = 384
SECS = 64
RADS = 8


def draw_neighbours(key, part):

    def one_block(block_key):
        key_local, key_order = jax.random.split(block_key)
        local_faces = jax.random.randint(key_local, (FACES, ELEMS), 0, ELEMS, dtype=jnp.int32)
        shuffled = jax.random.permutation(key_order, ELEMS)
        slots = ELEMS + jnp.arange(4 * BND, dtype=jnp.int32)
        first_face = local_faces[0].at[shuffled[:4 * BND]].set(slots)
        return local_faces.at[0].set(first_face)
    block_keys = jax.random.split(jax.random.fold_in(key, 17), SECS * RADS)
    drawn = jax.vmap(one_block)(block_keys)
    return drawn.reshape(SECS, RADS, FACES, ELEMS).astype(jnp.int32)


def draw_operator(key, part):
    key_skew, key_damp = jax.random.split(jax.random.fold_in(key, 29))
    gaussian = jax.random.normal(key_skew, (COMP, COMP), jnp.float32) / jnp.sqrt(COMP * 1.0)
    rotation = (gaussian - gaussian.T) / jnp.sqrt(2.0)
    damping = jnp.exp(jax.random.uniform(key_damp, (COMP,), jnp.float32, jnp.log(0.1), jnp.log(0.5)))
    return (rotation - jnp.diag(damping)).astype(jnp.float32)


def place_ends(values, key, smallest, high):
    extent = values.shape
    index_at = [jax.random.randint(jax.random.fold_in(key, axis), (), 0, extent[axis]) for axis in range(len(extent))]
    values = values.at[tuple(index_at)].set(smallest)
    longest = extent.index(max(extent))
    index_at[longest] = (index_at[longest] + 1) % extent[longest]
    return values.at[tuple(index_at)].set(high)


def level_of(rng, shape, cuts, low, high):
    def one(position, shards_of):
        steps = jax.random.uniform(jax.random.fold_in(jax.random.fold_in(rng, 6), position), (shards_of,), jnp.float32, low / len(cuts), high / len(cuts))
        return jnp.repeat(jnp.exp(steps), shape[position] // shards_of).reshape((-1,) + (1,) * (len(shape) - position - 1))

    loudness = one(*cuts[0])
    for cut in cuts[1:]:
        loudness = loudness * one(*cut)
    return loudness


def split_up(number_of, total, bound, lean):
    weights = [(1 << 20) // math.isqrt(rank ** lean) + 1 for rank in range(2, number_of + 1)]
    surplus, counts = total - bound - (number_of - 1), [1] * (number_of - 1)
    while surplus > 0:
        movable = [i for i in range(number_of - 1) if counts[i] < bound]
        whole, left = sum([weights[i] for i in movable]), surplus
        for i in movable:
            extra = min(bound - counts[i], max(1, left * weights[i] // whole), surplus)
            counts[i] = counts[i] + extra
            surplus = surplus - extra
    return np.array([bound] + counts)


def uneven_parts(own_key, number_of, total, bound, lean):
    if number_of == 2:
        one = jax.random.randint(own_key, (), max(1, total - bound), min(bound, total - 1) + 1)
        return jnp.stack([one, total - one])
    sizes = jnp.asarray(split_up(number_of, total, bound, lean), jnp.int32)
    twos = (number_of - 1) // 2
    source_of, sink = sizes[1:1 + 2 * twos:2], sizes[2:2 + 2 * twos:2]
    slack = jnp.minimum(source_of - 1, bound - sink)
    shifted = jax.random.randint(jax.random.fold_in(own_key, 1), (twos,), 0, 1 << 20) % (slack + 1)
    sizes = sizes.at[1:1 + 2 * twos:2].set(source_of - shifted).at[2:2 + 2 * twos:2].set(sink + shifted)
    return sizes[jax.random.permutation(jax.random.fold_in(own_key, 2), number_of)]


def bell_draw(own_key, dims, deviation, reach, cuts=(), kind=jnp.bfloat16):
    array = deviation * jax.random.normal(own_key, dims, jnp.float32)
    if cuts:
        array = array * level_of(own_key, dims, cuts, -0.22, 0.18)
    return jnp.clip(array, -reach, reach).astype(kind)


def setup_inputs(seed: int = 0) -> dict:
    keys = jax.random.split(jax.random.key(seed), 11)
    fields = bell_draw(keys[0], (SECS, RADS, COMP, ELEMS), 1.0, 6.0, ((0, 64), (1, 8)), jnp.float32)
    pattern = place_ends(jax.random.randint(keys[1], (SECS, RADS, ELEMS), 0, PATTERNS), jax.random.fold_in(keys[1], 1), 0, PATTERNS - 1).astype(jnp.int32)
    tent_order = jax.vmap(lambda own: jax.random.permutation(own, ELEMS))(jax.random.split(keys[2], SECS * RADS)).reshape((SECS, RADS, ELEMS)).astype(jnp.int32)
    level_sizes = jax.vmap(lambda own: uneven_parts(own, LEVELS, ELEMS, BLOCK, 1))(jax.random.split(keys[3], SECS * RADS)).reshape((SECS, RADS, LEVELS)).astype(jnp.int32)
    send_rows = place_ends(jax.random.randint(keys[4], (SECS, RADS, 4, BND), 0, ELEMS), jax.random.fold_in(keys[4], 1), 0, ELEMS - 1).astype(jnp.int32)
    neighbours = draw_neighbours(jax.random.fold_in(keys[10], 71), 0)
    operator = draw_operator(jax.random.fold_in(keys[10], 71), 0)
    trace_map = bell_draw(keys[7], (TRACE, COMP), COMP ** -0.5, 0.5, (), jnp.float32)
    lift_map = bell_draw(keys[8], (FACES, COMP, TRACE), (FACES * TRACE) ** -0.5, 0.375, (), jnp.float32)
    tent_height = jnp.clip(jnp.exp(jax.random.uniform(keys[9], (PATTERNS,), jnp.float32, math.log(0.15), math.log(0.5))), 0.15, 0.5)
    return {"fields": fields, "pattern": pattern, "tent_order": tent_order, "level_sizes": level_sizes, "send_rows": send_rows, "neighbours": neighbours, "operator": operator, "trace_map": trace_map, "lift_map": lift_map, "tent_height": tent_height}


precise = lax.Precision.HIGHEST


def propagate(loaded, heights, operator):
    for substep in range(SUBSTEPS):
        term_now = loaded
        summed = loaded
        for degree in range(1, TERMS + 1):
            term_now = jnp.dot(operator, term_now, precision=precise) * (heights / degree)
            summed = summed + term_now
        loaded = summed
    return loaded


def face_columns(source, faces_of):
    gathered = jnp.take(source, faces_of.reshape(-1), axis=1, mode="clip")
    gathered = gathered.reshape(source.shape[0], faces_of.shape[0], faces_of.shape[1])
    return jnp.transpose(gathered, (1, 0, 2)).reshape(-1, faces_of.shape[1])


def pick_rows(source, rows):
    picked = jnp.take(source, rows.reshape(-1), axis=1)
    return picked.reshape(source.shape[0], rows.shape[0], rows.shape[1])


def reference(fields, pattern, tent_order, level_sizes, send_rows, neighbours, operator, trace_map, lift_map, tent_height):
    heights_all = tent_height[pattern]
    starts = (jnp.cumsum(level_sizes, axis=-1) - level_sizes).astype(jnp.int32)
    tent_rows = jnp.concatenate([tent_order, jnp.zeros((SECS, RADS, BLOCK), jnp.int32)], axis=-1)
    lift_matrix = jnp.transpose(lift_map, (1, 0, 2)).reshape(lift_map.shape[1], -1)
    slot_ids = jnp.arange(BLOCK, dtype=jnp.int32)
    current = fields
    for level_index in range(LEVELS):
        outflow = jnp.einsum("tc,srce->srte", trace_map, current, precision=precise)
        outgoing = jax.vmap(jax.vmap(pick_rows))(outflow, send_rows)
        from_below = jnp.roll(outgoing[:, :, :, 0], 1, axis=0)
        from_above = jnp.roll(outgoing[:, :, :, 1], -1, axis=0)
        empty_rim = jnp.zeros_like(outgoing[:, :1, :, 2])
        inner_rim = jnp.concatenate([empty_rim, outgoing[:, :-1, :, 2]], axis=1)
        outer_rim = jnp.concatenate([outgoing[:, 1:, :, 3], empty_rim], axis=1)
        extended = jnp.concatenate([outflow, from_below, from_above, inner_rim, outer_rim], axis=-1)

        def advance(block_now, block_ext, block_faces, block_heights, block_rows, block_starts, block_counts):
            members = lax.dynamic_slice_in_dim(block_rows, block_starts[level_index], BLOCK)
            filled = slot_ids < block_counts[level_index]
            columns = jnp.take(block_now, members, axis=1)
            faces_of = jnp.take(block_faces, members, axis=1)
            loaded = columns + jnp.dot(lift_matrix, face_columns(block_ext, faces_of), precision=precise)
            loaded = propagate(loaded, jnp.take(block_heights, members), operator)
            target = jnp.where(filled, members, block_now.shape[1])
            return block_now.at[:, target].set(loaded, mode="drop")

        current = jax.vmap(jax.vmap(advance))(current, extended, neighbours, heights_all, tent_rows, starts, level_sizes)
    return current
```

```python
import functools

import jax
import jax.numpy as jnp
import numpy as np
from jax import lax
from jax.experimental import pallas as pl
from jax.experimental.pallas import tpu as pltpu
from jax.sharding import PartitionSpec as P

LEVELS = 4
FACES = 4
SUBSTEPS = 2
TERMS = 4
BLOCK = 384
ELEMS = 1024
COMP = 140
TRACE = 60
BND = 128
CP = 144
TP = 64
LOCAL = LEVELS * BLOCK
KB = 256

MESH = pl.DeviceIdType.MESH
F32 = jnp.float32
BF16 = jnp.bfloat16
I32 = jnp.int32


def substep_powers():
    one = np.array([1.0 / np.prod(np.arange(1, k + 1)) for k in range(TERMS + 1)])
    total = np.array([1.0])
    for _ in range(SUBSTEPS):
        total = np.convolve(total, one)
    return [float(c) for c in total]


COEF = substep_powers()
DEG = SUBSTEPS * TERMS


def hi_lo(x):
    hi = x.astype(BF16)
    return hi, (x - hi.astype(F32)).astype(BF16)


def right3(x):
    hi, lo = hi_lo(x)
    return jnp.concatenate([hi, hi, lo], axis=0)


def left3(m):
    hi, lo = hi_lo(m)
    return jnp.concatenate([hi, lo, hi], axis=1)


def dot(a, b):
    return jnp.dot(a, b, preferred_element_type=F32)


def dot_exact(a, b):
    return jnp.dot(a, b, precision=lax.Precision.HIGHEST, preferred_element_type=F32)


def one_hot(row, depth):
    n = row.shape[1]
    line = lax.broadcasted_iota(I32, (depth, n), 0)
    return jnp.where(line == jnp.broadcast_to(row, (depth, n)), 1.0, 0.0).astype(BF16)


def look_up(table, index):
    lane = index & 127
    tile = index >> 7
    out = jnp.zeros(index.shape, table.dtype)
    for m in range(table.shape[1] // 128):
        part = jnp.broadcast_to(table[:, 128 * m : 128 * m + 128], index.shape)
        got = jnp.take_along_axis(part, lane, axis=1, mode="promise_in_bounds")
        out = jnp.where(tile == m, got, out)
    return out


def kernel(
    secs,
    rads,
    fields,
    pattern,
    order,
    sizes,
    neighbours,
    sends,
    operator,
    trace_map,
    lift_map,
    tent_height,
    out,
    xp,
    tp,
    ap,
    lp,
    t3,
    a3,
    l3,
    ohin,
    pos_ref,
    sx_ref,
    nbx_ref,
    h_ref,
    state,
    flow,
    gath,
    loaded_ref,
    sb,
    rb,
    send_sem,
    recv_sem,
):
    s = lax.axis_index("sector")
    r = lax.axis_index("radial")
    up = lax.rem(s + 1, secs)
    down = lax.rem(s + secs - 1, secs)

    barrier = pltpu.get_barrier_semaphore()

    def greet(a, b):
        pl.semaphore_signal(barrier, inc=1, device_id=(a, b), device_id_type=MESH)

    greet(up, r)
    greet(down, r)

    @pl.when(r > 0)
    def _():
        greet(s, r - 1)

    @pl.when(r < rads - 1)
    def _():
        greet(s, r + 1)

    @pl.when(r == 0)
    def _():
        rb[:, 2] = jnp.zeros((LEVELS, TP, BND), F32)

    @pl.when(r == rads - 1)
    def _():
        rb[:, 3] = jnp.zeros((LEVELS, TP, BND), F32)

    def copy(level, group, a, b):
        return pltpu.make_async_remote_copy(
            src_ref=sb.at[level, group],
            dst_ref=rb.at[level, group],
            send_sem=send_sem.at[level, group],
            recv_sem=recv_sem.at[level, group],
            device_id=(a, b),
            device_id_type=MESH,
        )

    def start(level):
        @pl.when(r < rads - 1)
        def _():
            copy(level, 2, s, r + 1).start()

        @pl.when(r > 0)
        def _():
            copy(level, 3, s, r - 1).start()

        copy(level, 0, up, r).start()
        copy(level, 1, down, r).start()

    def arrive(level):
        copy(level, 0, up, r).wait_recv()
        copy(level, 1, down, r).wait_recv()

        @pl.when(r > 0)
        def _():
            copy(level, 2, s, r - 1).wait_recv()

        @pl.when(r < rads - 1)
        def _():
            copy(level, 3, s, r + 1).wait_recv()

    def drain(level):
        copy(level, 0, up, r).wait_send()
        copy(level, 1, down, r).wait_send()

        @pl.when(r < rads - 1)
        def _():
            copy(level, 2, s, r + 1).wait_send()

        @pl.when(r > 0)
        def _():
            copy(level, 3, s, r - 1).wait_send()

    def fill_sends(level, got):
        for d in range(4):
            part = got[:, BND * d : BND * d + BND]
            sb[level, d] = part[:TP] + part[TP:]

    tp[...] = jnp.zeros((TP, CP), F32)
    tp[0:TRACE, 0:COMP] = trace_map[...]
    t3[0:TP] = left3(tp[...])
    xp[0:COMP] = fields[...]
    xp[COMP:CP] = jnp.zeros((CP - COMP, ELEMS), F32)
    first = dot(t3[0:TP], right3(xp[...]))
    first_hl = jnp.concatenate(hi_lo(first), axis=0)
    got = jnp.zeros((2 * TP, 4 * BND), F32)
    for m in range(ELEMS // KB):
        got += dot(first_hl[:, KB * m : KB * m + KB], one_hot(sends[...] - KB * m, KB))
    fill_sends(0, got)
    pl.semaphore_wait(
        barrier, 2 + jnp.where(r > 0, 1, 0) + jnp.where(r < rads - 1, 1, 0)
    )
    start(0)

    ap[...] = jnp.zeros((CP, CP), F32)
    ap[0:COMP, 0:COMP] = operator[...]
    p1 = ap[...]
    p2 = dot_exact(p1, p1)
    p12 = jnp.concatenate([p1, p2], axis=0)
    p34 = dot_exact(p12, p2)
    p4 = p34[CP:]
    p14 = jnp.concatenate([p12, p34], axis=0)
    p58 = dot_exact(p14, p4)
    a3[0 : 4 * CP] = left3(p14)
    a3[4 * CP :] = left3(p58)
    q0 = tp[...]
    q1 = dot_exact(q0, p1)
    q01 = jnp.concatenate([q0, q1], axis=0)
    q23 = dot_exact(q01, p2)
    q03 = jnp.concatenate([q01, q23], axis=0)
    q47 = dot_exact(q03, p4)
    q8 = dot_exact(q47[:TP], p4)
    t3[TP:] = left3(jnp.concatenate([q1, q23, q47, q8], axis=0))
    lp[...] = jnp.zeros((CP, FACES * TP), F32)
    for f in range(FACES):
        lp[0:COMP, TP * f : TP * f + TRACE] = lift_map[f]
    l3[...] = left3(lp[...])

    line = lax.broadcasted_iota(I32, (16, 128), 0)
    lane = lax.broadcasted_iota(I32, (16, 128), 1)
    shift = jnp.zeros((16, 128), I32)
    limit = jnp.zeros((16, 128), I32)
    begin = jnp.int32(0)
    for l in range(LEVELS):
        size = sizes[l]
        mine = (line >= 3 * l) & (line < 3 * l + 3)
        shift = jnp.where(mine, begin - BLOCK * l, shift)
        limit = jnp.where(mine, BLOCK * l + size, limit)
        begin = begin + size
    slot = 128 * line + lane
    place = jnp.minimum(jnp.maximum(slot + shift, 0), ELEMS - 1)
    element = jnp.where(slot < limit, look_up(order[...], place), -1)
    for l in range(LEVELS):
        row = jnp.concatenate([element[3 * l + t : 3 * l + t + 1] for t in range(3)], axis=1)
        for m in range(ELEMS // KB):
            ohin[l, KB * m : KB * m + KB] = one_hot(row - KB * m, KB)

    line = lax.broadcasted_iota(I32, (16, BLOCK), 0)
    lane = lax.broadcasted_iota(I32, (16, BLOCK), 1)
    pos = jnp.zeros((16, ELEMS), F32)
    for l in range(LEVELS):
        number = lane + BLOCK * l
        digits = jnp.where(line == 0, number >> 8, jnp.where(line == 1, number & 255, 0))
        pos += lax.dot_general(
            digits.astype(F32).astype(BF16),
            ohin[l],
            (((1,), (1,)), ((), ())),
            preferred_element_type=F32,
        )
    pos = pos.astype(I32)
    pos = pos[0:1] * 256 + pos[1:2]
    pos_ref[...] = pos

    wide = []
    for t in range(ELEMS // 128):
        part = neighbours[:, 128 * t : 128 * t + 128]
        inside = look_up(pos, jnp.minimum(part, ELEMS - 1))
        wide.append(jnp.where(part < ELEMS, inside, part + (LOCAL - ELEMS)))
    wide = jnp.concatenate(wide, axis=1)
    for d in range(4):
        sx_ref[:, BND * d : BND * d + BND] = look_up(
            pos, jnp.broadcast_to(sends[:, BND * d : BND * d + BND], (8, BND))
        )[0:1]

    line = lax.broadcasted_iota(I32, (8, ELEMS), 0)
    extra = jnp.where(line == 0, jnp.broadcast_to(pattern[...], (8, ELEMS)), 0)
    index_rows = jnp.concatenate([wide >> 8, wide & 255, extra], axis=0)
    xhi, xlo = hi_lo(xp[...])
    rows = jnp.concatenate([xhi, xlo, index_rows.astype(F32).astype(BF16)], axis=0)
    for l in range(LEVELS):
        moved = dot(rows, ohin[l])
        x = moved[:CP] + moved[CP : 2 * CP]
        state[l] = x
        numbers = moved[2 * CP :].astype(I32)
        nbx_ref[l] = numbers[0:4] * 256 + numbers[4:8]
        kind = numbers[8:9]
        height = jnp.zeros((1, BLOCK), F32)
        for p in range(16):
            height = jnp.where(kind == p, tent_height[p], height)
        h_ref[l] = height
        o = dot(t3[0:TP], right3(x))
        flow[:, BLOCK * l : BLOCK * l + BLOCK] = jnp.concatenate(hi_lo(o), axis=0)
    out[...] = jnp.zeros((COMP, ELEMS), F32)

    def weights(l):
        h = h_ref[l]
        power = jnp.ones_like(h)
        ws = []
        for k in range(1, DEG + 1):
            power = power * h
            ws.append(power * COEF[k])
        return ws

    def finish(l):
        x = loaded_ref[...]
        x3 = right3(x)
        y = x
        ws = weights(l)
        for k in range(1, DEG + 1):
            y += dot(a3[CP * (k - 1) : CP * k], x3) * ws[k - 1]
        hl = jnp.concatenate(hi_lo(y), axis=0)
        for n in range(ELEMS // KB):
            row = pos_ref[:, KB * n : KB * n + KB] - BLOCK * l
            got = dot(hl, one_hot(row, BLOCK))
            out[:, KB * n : KB * n + KB] += got[:COMP] + got[CP : CP + COMP]

    def level(l, carry):
        @pl.when(l > 0)
        def _():
            finish(l - 1)

        for f in range(FACES):
            row = nbx_ref[l, f : f + 1]
            acc = jnp.zeros((2 * TP, BLOCK), F32)
            for m in range(LOCAL // KB):
                acc += dot(flow[:, KB * m : KB * m + KB], one_hot(row - KB * m, KB))
            gath[f] = acc
        arrive(l)
        for d in range(4):
            hi, lo = hi_lo(rb[l, d])
            flow[:, LOCAL + BND * d : LOCAL + BND * d + BND] = jnp.concatenate([hi, lo], axis=0)
        his, los = [], []
        for f in range(FACES):
            row = nbx_ref[l, f : f + 1]
            acc = gath[f]
            for m in range(LOCAL // KB, (LOCAL + 4 * BND) // KB):
                acc += dot(flow[:, KB * m : KB * m + KB], one_hot(row - KB * m, KB))
            acc = acc.astype(BF16)
            his.append(acc[:TP])
            los.append(acc[TP:])
        x = state[l] + dot(l3[...], jnp.concatenate(his + his + los, axis=0))
        loaded_ref[...] = x

        @pl.when(l < LEVELS - 1)
        def _():
            x3 = right3(x)
            ws = weights(l)
            o = dot(t3[0:TP], x3)
            for k in range(1, DEG + 1):
                o += dot(t3[TP * k : TP * k + TP], x3) * ws[k - 1]
            here = pl.ds(pl.multiple_of(BLOCK * l, 128), BLOCK)
            flow[:, here] = jnp.concatenate(hi_lo(o), axis=0)
            got = jnp.zeros((2 * TP, 4 * BND), F32)
            for m in range(LOCAL // KB):
                got += dot(flow[:, KB * m : KB * m + KB], one_hot(sx_ref[...] - KB * m, KB))
            fill_sends(l + 1, got)
            start(l + 1)

        return carry

    lax.fori_loop(0, LEVELS, level, 0)
    finish(LEVELS - 1)
    for l in range(LEVELS):
        drain(l)


def solution(mesh):
    secs, rads = mesh.shape["sector"], mesh.shape["radial"]
    vmem = pl.BlockSpec(memory_space=pltpu.VMEM)
    smem = pl.BlockSpec(memory_space=pltpu.SMEM)

    def body(
        fields,
        pattern,
        tent_order,
        level_sizes,
        send_rows,
        neighbours,
        operator,
        trace_map,
        lift_map,
        tent_height,
    ):
        out = pl.pallas_call(
            functools.partial(kernel, secs, rads),
            out_shape=jax.ShapeDtypeStruct((COMP, ELEMS), F32),
            in_specs=[vmem, vmem, vmem, smem, vmem, vmem, vmem, vmem, vmem, smem],
            out_specs=vmem,
            scratch_shapes=[
                pltpu.VMEM((CP, ELEMS), F32),
                pltpu.VMEM((TP, CP), F32),
                pltpu.VMEM((CP, CP), F32),
                pltpu.VMEM((CP, FACES * TP), F32),
                pltpu.VMEM(((DEG + 1) * TP, 3 * CP), BF16),
                pltpu.VMEM((DEG * CP, 3 * CP), BF16),
                pltpu.VMEM((CP, 3 * FACES * TP), BF16),
                pltpu.VMEM((LEVELS, ELEMS, BLOCK), BF16),
                pltpu.VMEM((1, ELEMS), I32),
                pltpu.VMEM((1, 4 * BND), I32),
                pltpu.VMEM((LEVELS, 4, BLOCK), I32),
                pltpu.VMEM((LEVELS, 1, BLOCK), F32),
                pltpu.VMEM((LEVELS, CP, BLOCK), F32),
                pltpu.VMEM((2 * TP, LOCAL + 4 * BND), BF16),
                pltpu.VMEM((FACES, 2 * TP, BLOCK), F32),
                pltpu.VMEM((CP, BLOCK), F32),
                pltpu.VMEM((LEVELS, 4, TP, BND), F32),
                pltpu.VMEM((LEVELS, 4, TP, BND), F32),
                pltpu.SemaphoreType.DMA((LEVELS, 4)),
                pltpu.SemaphoreType.DMA((LEVELS, 4)),
            ],
            compiler_params=pltpu.CompilerParams(
                collective_id=0, has_side_effects=True, vmem_limit_bytes=60 * 2**20
            ),
            name="tent_layer",
        )(
            fields[0, 0],
            pattern[0],
            tent_order[0],
            level_sizes[0, 0],
            neighbours[0, 0],
            send_rows.reshape(1, 4 * BND),
            operator,
            trace_map,
            lift_map,
            tent_height,
        )
        return out[None, None]

    block = P("sector", "radial", None)
    wide = P("sector", "radial", None, None)
    return jax.shard_map(
        body,
        mesh=mesh,
        in_specs=(wide, block, block, block, wide, wide, P(), P(), P(), P()),
        out_specs=wide,
        check_vma=False,
    )
```

```python
import functools

import jax
import jax.numpy as jnp
import numpy as np
from jax import lax
from jax.experimental import pallas as pl
from jax.experimental.pallas import tpu as pltpu
from jax.sharding import PartitionSpec as P

LEVELS = 4
FACES = 4
SUBSTEPS = 2
TERMS = 4
BLOCK = 384
ELEMS = 1024
COMP = 140
TRACE = 60
BND = 128
CP = 144
TP = 64
SLOTS = 4 * BND
CHUNKS = 5
KB = 256

MESH = pl.DeviceIdType.MESH
F32 = jnp.float32
BF16 = jnp.bfloat16
I32 = jnp.int32


def substep_powers():
    one = np.array([1.0 / np.prod(np.arange(1, k + 1)) for k in range(TERMS + 1)])
    total = np.array([1.0])
    for _ in range(SUBSTEPS):
        total = np.convolve(total, one)
    return [float(c) for c in total]


COEF = substep_powers()
DEG = SUBSTEPS * TERMS


def hi_lo(x):
    hi = x.astype(BF16)
    return hi, (x - hi.astype(F32)).astype(BF16)


def right3(x):
    hi, lo = hi_lo(x)
    return jnp.concatenate([hi, hi, lo], axis=0)


def left3(m):
    hi, lo = hi_lo(m)
    return jnp.concatenate([hi, lo, hi], axis=1)


def dot(a, b):
    return jnp.dot(a, b, preferred_element_type=F32)


def one_hot(row, depth):
    n = row.shape[1]
    line = lax.broadcasted_iota(I32, (depth, n), 0)
    return jnp.where(line == jnp.broadcast_to(row, (depth, n)), 1.0, 0.0).astype(BF16)


def look_up(table, index):
    lane = index & 127
    tile = index >> 7
    out = jnp.zeros(index.shape, table.dtype)
    for m in range(table.shape[1] // 128):
        part = jnp.broadcast_to(table[:, 128 * m : 128 * m + 128], index.shape)
        got = jnp.take_along_axis(part, lane, axis=1, mode="promise_in_bounds")
        out = jnp.where(tile == m, got, out)
    return out


def kernel(
    secs,
    rads,
    fields_hbm,
    pattern_hbm,
    order_hbm,
    sizes_hbm,
    neighbours_hbm,
    sends_hbm,
    operator_hbm,
    trace_hbm,
    lift_hbm,
    heights_hbm,
    out,
    fields,
    pattern,
    order,
    sizes,
    neighbours,
    sends,
    operator,
    trace_map,
    lift_map,
    tent_height,
    in_sem,
    xp,
    tp,
    ap,
    lp,
    t3,
    a3,
    l3,
    rows,
    erow,
    ecol,
    scatter,
    pick,
    catch,
    nbx,
    height,
    start_x,
    flow,
    fresh,
    part,
    gath,
    loaded,
    sb,
    rb,
    send_sem,
    recv_sem,
):
    s = lax.axis_index("sector")
    r = lax.axis_index("radial")
    up = lax.rem(s + 1, secs)
    down = lax.rem(s + secs - 1, secs)

    step = COMP * 8 // CHUNKS
    pieces = [pl.ds(step * c, step) for c in range(CHUNKS)]
    loads = [
        pltpu.make_async_copy(src, dst, in_sem.at[i])
        for i, (src, dst) in enumerate(
            [(trace_hbm, trace_map)]
            + [(fields_hbm.at[p], fields.at[p]) for p in pieces]
            + [
                (sends_hbm, sends),
                (operator_hbm, operator),
                (order_hbm, order),
                (sizes_hbm, sizes),
                (neighbours_hbm, neighbours),
                (pattern_hbm, pattern),
                (heights_hbm, tent_height),
                (lift_hbm, lift_map),
            ]
        )
    ]
    for load in loads:
        load.start()

    barrier = pltpu.get_barrier_semaphore()

    def greet(a, b):
        pl.semaphore_signal(barrier, inc=1, device_id=(a, b), device_id_type=MESH)

    greet(up, r)
    greet(down, r)

    @pl.when(r > 0)
    def _():
        greet(s, r - 1)

    @pl.when(r < rads - 1)
    def _():
        greet(s, r + 1)

    @pl.when(r == 0)
    def _():
        rb[:, 2] = jnp.zeros((LEVELS, TP, BND), F32)

    @pl.when(r == rads - 1)
    def _():
        rb[:, 3] = jnp.zeros((LEVELS, TP, BND), F32)

    def copy(level, group, a, b):
        return pltpu.make_async_remote_copy(
            src_ref=sb.at[level, group],
            dst_ref=rb.at[level, group],
            send_sem=send_sem.at[level, group],
            recv_sem=recv_sem.at[level, group],
            device_id=(a, b),
            device_id_type=MESH,
        )

    def start(level):
        @pl.when(r < rads - 1)
        def _():
            copy(level, 2, s, r + 1).start()

        @pl.when(r > 0)
        def _():
            copy(level, 3, s, r - 1).start()

        copy(level, 0, up, r).start()
        copy(level, 1, down, r).start()

    def arrive(level):
        copy(level, 0, up, r).wait_recv()
        copy(level, 1, down, r).wait_recv()

        @pl.when(r > 0)
        def _():
            copy(level, 2, s, r - 1).wait_recv()

        @pl.when(r < rads - 1)
        def _():
            copy(level, 3, s, r + 1).wait_recv()

    def drain(level):
        copy(level, 0, up, r).wait_send()
        copy(level, 1, down, r).wait_send()

        @pl.when(r < rads - 1)
        def _():
            copy(level, 2, s, r + 1).wait_send()

        @pl.when(r > 0)
        def _():
            copy(level, 3, s, r - 1).wait_send()

    def fill_sends(level, got):
        for d in range(4):
            piece = got[:, BND * d : BND * d + BND]
            sb[level, d] = piece[:TP] + piece[TP:]

    tp[...] = jnp.zeros((TP, CP), F32)
    xp[COMP:CP] = jnp.zeros((CP - COMP, ELEMS), F32)
    loads[0].wait()
    tp[0:TRACE, 0:COMP] = trace_map[...]
    t3[0:TP] = left3(tp[...])
    for load in loads[1 : CHUNKS + 1]:
        load.wait()
    for t in range(ELEMS // 128):
        xp[0:COMP, 128 * t : 128 * t + 128] = fields[pl.ds(t, COMP, stride=8)]
    hi, lo = hi_lo(xp[...])
    rows[0:CP] = hi
    rows[CP : 2 * CP] = lo
    first = dot(t3[0:TP], jnp.concatenate([hi, hi, lo], axis=0))
    flow[:, 0:ELEMS] = jnp.concatenate(hi_lo(first), axis=0)
    rest = loads[CHUNKS + 1 :]
    rest[0].wait()
    got = jnp.zeros((2 * TP, SLOTS), F32)
    for m in range(ELEMS // KB):
        got += dot(flow[:, KB * m : KB * m + KB], one_hot(sends[...] - KB * m, KB))
    fill_sends(0, got)
    pl.semaphore_wait(
        barrier, 2 + jnp.where(r > 0, 1, 0) + jnp.where(r < rads - 1, 1, 0)
    )
    start(0)

    ap[...] = jnp.zeros((CP, CP), F32)
    lp[...] = jnp.zeros((FACES * TP, 256), F32)
    rest[1].wait()
    ap[0:COMP, 0:COMP] = operator[...]
    p1 = ap[...]
    a3[0:CP] = left3(p1)
    b1 = right3(p1)
    p2 = dot(a3[0:CP], b1)
    a3[CP : 2 * CP] = left3(p2)
    b2 = right3(p2)
    p34 = dot(a3[0 : 2 * CP], b2)
    a3[2 * CP : 4 * CP] = left3(p34)
    b4 = right3(p34[CP:])
    a3[4 * CP : 8 * CP] = left3(dot(a3[0 : 4 * CP], b4))
    t3[TP : 2 * TP] = left3(dot(t3[0:TP], b1))
    t3[2 * TP : 4 * TP] = left3(dot(t3[0 : 2 * TP], b2))
    t3[4 * TP : 8 * TP] = left3(dot(t3[0 : 4 * TP], b4))
    t3[8 * TP : 9 * TP] = left3(dot(t3[4 * TP : 5 * TP], b4))

    for load in rest[2:7]:
        load.wait()
    line = lax.broadcasted_iota(I32, (16, 128), 0)
    lane = lax.broadcasted_iota(I32, (16, 128), 1)
    shift = jnp.zeros((16, 128), I32)
    limit = jnp.zeros((16, 128), I32)
    begin = jnp.int32(0)
    for l in range(LEVELS):
        size = sizes[l]
        mine = (line >= 3 * l) & (line < 3 * l + 3)
        shift = jnp.where(mine, begin - BLOCK * l, shift)
        limit = jnp.where(mine, BLOCK * l + size, limit)
        begin = begin + size
    slot = 128 * line + lane
    place = jnp.minimum(jnp.maximum(slot + shift, 0), ELEMS - 1)
    element = jnp.where(slot < limit, look_up(order[...], place), -1)
    tall = jnp.concatenate([element.astype(F32), jnp.zeros((112, 128), F32)], axis=0)
    tall = jnp.transpose(tall)
    for l in range(LEVELS):
        for t in range(3):
            n = 3 * l + t
            erow[l, :, 128 * t : 128 * t + 128] = element[n : n + 1]
            ecol[l, 128 * t : 128 * t + 128] = jnp.broadcast_to(tall[:, n : n + 1], (128, 128))
    line = lax.broadcasted_iota(I32, (8, ELEMS), 0)
    extra = jnp.where(line == 0, jnp.broadcast_to(pattern[...], (8, ELEMS)), 0)
    near = neighbours[...]
    numbers = jnp.concatenate([near >> 8, near & 255, extra], axis=0)
    rows[2 * CP :] = numbers.astype(F32).astype(BF16)
    rest[7].wait()
    for f in range(FACES):
        lp[TP * f : TP * f + TRACE, 0:COMP] = lift_map[:, f]
    l3[...] = left3(jnp.transpose(lp[...])[0:CP])
    out[...] = jnp.zeros((COMP * 8, 128), F32)

    def weights(l):
        h = height[l]
        power = jnp.ones_like(h)
        ws = []
        for k in range(1, DEG + 1):
            power = power * h
            ws.append(power * COEF[k])
        return ws

    def finish(l):
        x = loaded[...]
        x3 = right3(x)
        y = x
        ws = weights(l)
        for k in range(1, DEG + 1):
            y += dot(a3[CP * (k - 1) : CP * k], x3) * ws[k - 1]
        hl = jnp.concatenate(hi_lo(y), axis=0)
        for n in range(ELEMS // KB):
            here = slice(KB * n, KB * n + KB)
            got = dot(hl, scatter[:, here])
            got = got[:COMP] + got[CP : CP + COMP]
            for t in range(KB // 128):
                place = pl.ds(n * (KB // 128) + t, COMP, stride=8)
                out[place] += got[:, 128 * t : 128 * t + 128]

    def level(l, carry):
        @pl.when(l > 0)
        def _():
            finish(l - 1)
            for n in range(ELEMS // KB):
                here = slice(KB * n, KB * n + KB)
                flow[:, here] += dot(fresh[...], scatter[:, here]).astype(BF16)

        moved = jnp.zeros((2 * CP + 16, BLOCK), F32)
        for m in range(ELEMS // KB):
            moved += dot(rows[:, KB * m : KB * m + KB], one_hot(erow[l] - KB * m, KB))
        start_x[...] = moved[:CP] + moved[CP : 2 * CP]
        numbers = moved[2 * CP :].astype(I32)
        nbx[...] = numbers[0:4] * 256 + numbers[4:8]
        kind = numbers[8:9]
        h = jnp.zeros((1, BLOCK), F32)
        for p in range(16):
            h = jnp.where(kind == p, tent_height[p], h)
        height[l] = h
        for f in range(FACES):
            row = nbx[f : f + 1]
            acc = jnp.zeros((2 * TP, BLOCK), F32)
            for m in range(ELEMS // KB):
                acc += dot(flow[:, KB * m : KB * m + KB], one_hot(row - KB * m, KB))
            gath[f] = acc
            catch[:, BLOCK * f : BLOCK * f + BLOCK] = one_hot(row - ELEMS, SLOTS)
        for t in range(ELEMS // 128):
            row = lax.broadcasted_iota(I32, (BLOCK, 128), 1).astype(F32) + 128.0 * t
            hit = jnp.where(ecol[l] == row, 1.0, 0.0).astype(BF16)
            scatter[:, 128 * t : 128 * t + 128] = hit

        @pl.when(l < LEVELS - 1)
        def _():
            gone = dot(jnp.ones((16, BLOCK), BF16), scatter[...])[0:1]
            keep = jnp.broadcast_to(1.0 - gone, (2 * TP, ELEMS))
            flow[:, 0:ELEMS] = (flow[:, 0:ELEMS].astype(F32) * keep).astype(BF16)
            got = jnp.zeros((2 * TP, SLOTS), F32)
            for m in range(ELEMS // KB):
                got += dot(flow[:, KB * m : KB * m + KB], one_hot(sends[...] - KB * m, KB))
            part[...] = got
            for d in range(4):
                row = sends[:, BND * d : BND * d + BND].astype(F32)
                hit = jnp.where(ecol[l] == jnp.broadcast_to(row, (BLOCK, BND)), 1.0, 0.0)
                pick[:, BND * d : BND * d + BND] = hit.astype(BF16)

        arrive(l)
        come = jnp.concatenate([rb[l, d] for d in range(4)], axis=1)
        come = dot(jnp.concatenate(hi_lo(come), axis=0), catch[...])
        his, los = [], []
        for f in range(FACES):
            acc = (gath[f] + come[:, BLOCK * f : BLOCK * f + BLOCK]).astype(BF16)
            his.append(acc[:TP])
            los.append(acc[TP:])
        x = start_x[...] + dot(l3[...], jnp.concatenate(his + his + los, axis=0))
        loaded[...] = x

        @pl.when(l < LEVELS - 1)
        def _():
            x3 = right3(x)
            ws = weights(l)
            o = dot(t3[0:TP], x3)
            for k in range(1, DEG + 1):
                o += dot(t3[TP * k : TP * k + TP], x3) * ws[k - 1]
            o = jnp.concatenate(hi_lo(o), axis=0)
            fresh[...] = o
            fill_sends(l + 1, part[...] + dot(o, pick[...]))
            start(l + 1)

        return carry

    lax.fori_loop(0, LEVELS, level, 0)
    finish(LEVELS - 1)
    for l in range(LEVELS):
        drain(l)


def solution(mesh):
    secs, rads = mesh.shape["sector"], mesh.shape["radial"]
    hbm = pl.BlockSpec(memory_space=pltpu.HBM)

    def body(
        fields,
        pattern,
        tent_order,
        level_sizes,
        send_rows,
        neighbours,
        operator,
        trace_map,
        lift_map,
        tent_height,
    ):
        args = (
            fields.reshape(COMP * 8, 128),
            pattern[0],
            tent_order[0],
            level_sizes[0, 0],
            neighbours[0, 0],
            send_rows.reshape(1, SLOTS),
            operator,
            trace_map,
            jnp.transpose(lift_map, (2, 0, 1)),
            tent_height,
        )
        args = tuple(pltpu.with_memory_space_constraint(a, pltpu.HBM) for a in args)
        homes = [
            (pltpu.SMEM if len(a.shape) == 1 else pltpu.VMEM)(a.shape, a.dtype) for a in args
        ]
        out = pl.pallas_call(
            functools.partial(kernel, secs, rads),
            out_shape=jax.ShapeDtypeStruct((COMP * 8, 128), F32),
            in_specs=[hbm] * len(args),
            out_specs=pl.BlockSpec(memory_space=pltpu.VMEM),
            scratch_shapes=homes
            + [
                pltpu.SemaphoreType.DMA((len(args) - 1 + CHUNKS,)),
                pltpu.VMEM((CP, ELEMS), F32),
                pltpu.VMEM((TP, CP), F32),
                pltpu.VMEM((CP, CP), F32),
                pltpu.VMEM((FACES * TP, 256), F32),
                pltpu.VMEM(((DEG + 1) * TP, 3 * CP), BF16),
                pltpu.VMEM((DEG * CP, 3 * CP), BF16),
                pltpu.VMEM((CP, 3 * FACES * TP), BF16),
                pltpu.VMEM((2 * CP + 16, ELEMS), BF16),
                pltpu.VMEM((LEVELS, 1, BLOCK), I32),
                pltpu.VMEM((LEVELS, BLOCK, 128), F32),
                pltpu.VMEM((BLOCK, ELEMS), BF16),
                pltpu.VMEM((BLOCK, SLOTS), BF16),
                pltpu.VMEM((SLOTS, FACES * BLOCK), BF16),
                pltpu.VMEM((FACES, BLOCK), I32),
                pltpu.VMEM((LEVELS, 1, BLOCK), F32),
                pltpu.VMEM((CP, BLOCK), F32),
                pltpu.VMEM((2 * TP, ELEMS), BF16),
                pltpu.VMEM((2 * TP, BLOCK), BF16),
                pltpu.VMEM((2 * TP, SLOTS), F32),
                pltpu.VMEM((FACES, 2 * TP, BLOCK), F32),
                pltpu.VMEM((CP, BLOCK), F32),
                pltpu.VMEM((LEVELS, 4, TP, BND), F32),
                pltpu.VMEM((LEVELS, 4, TP, BND), F32),
                pltpu.SemaphoreType.DMA((LEVELS, 4)),
                pltpu.SemaphoreType.DMA((LEVELS, 4)),
            ],
            compiler_params=pltpu.CompilerParams(
                collective_id=0, has_side_effects=True, vmem_limit_bytes=32 * 2**20
            ),
            name="tent_layer",
        )(*args)
        return out.reshape(1, 1, COMP, ELEMS)

    block = P("sector", "radial", None)
    wide = P("sector", "radial", None, None)
    return jax.shard_map(
        body,
        mesh=mesh,
        in_specs=(wide, block, block, block, wide, wide, P(), P(), P(), P()),
        out_specs=wide,
        check_vma=False,
    )
```

```python
import functools

import jax
import jax.numpy as jnp
import numpy as np
from jax import lax
from jax.experimental import pallas as pl
from jax.experimental.pallas import tpu as pltpu
from jax.sharding import PartitionSpec as P

LEVELS = 4
FACES = 4
SUBSTEPS = 2
TERMS = 4
BLOCK = 384
ELEMS = 1024
COMP = 140
TRACE = 60
BND = 128
CP = 144
TP = 64
SLOTS = 4 * BND
TILES = ELEMS // 128
KB = 256

MESH = pl.DeviceIdType.MESH
F32 = jnp.float32
BF16 = jnp.bfloat16
I32 = jnp.int32


def substep_powers():
    one = np.array([1.0 / np.prod(np.arange(1, k + 1)) for k in range(TERMS + 1)])
    total = np.array([1.0])
    for _ in range(SUBSTEPS):
        total = np.convolve(total, one)
    return [float(c) for c in total]


COEF = substep_powers()
DEG = SUBSTEPS * TERMS
HALF = DEG // 2


def hi_lo(x):
    hi = x.astype(BF16)
    return hi, (x - hi.astype(F32)).astype(BF16)


def right3(x):
    hi, lo = hi_lo(x)
    return jnp.concatenate([hi, hi, lo], axis=0)


def left3(m):
    hi, lo = hi_lo(m)
    return jnp.concatenate([hi, lo, hi], axis=1)


def dot(a, b):
    return jnp.dot(a, b, preferred_element_type=F32)


def one_hot(row, base):
    n = row.shape[1]
    line = lax.broadcasted_iota(I32, (KB, n), 0).astype(F32).astype(BF16)
    row = jnp.minimum(jnp.maximum(row - base, -1), KB).astype(F32).astype(BF16)
    return jnp.where(line == jnp.broadcast_to(row, (KB, n)), jnp.bfloat16(1), jnp.bfloat16(0))


def look_up(table, index):
    lane = index & 127
    tile = index >> 7
    out = jnp.zeros(index.shape, table.dtype)
    for m in range(table.shape[1] // 128):
        part = jnp.broadcast_to(table[:, 128 * m : 128 * m + 128], index.shape)
        got = jnp.take_along_axis(part, lane, axis=1, mode="promise_in_bounds")
        out = jnp.where(tile == m, got, out)
    return out


def kernel(
    secs,
    rads,
    fields_hbm,
    pattern_hbm,
    order_hbm,
    sizes_hbm,
    neighbours_hbm,
    sends_hbm,
    operator_hbm,
    trace_hbm,
    lift_hbm,
    heights_hbm,
    out,
    fields,
    pattern,
    order,
    sizes,
    neighbours,
    sends,
    operator,
    trace_map,
    lift_map,
    tent_height,
    in_sem,
    tp,
    ap,
    lp,
    t3,
    a3,
    l3,
    rows,
    erow,
    ecol,
    scatter,
    pick,
    listed,
    catch,
    nbx,
    height,
    start_x,
    flow,
    fresh,
    part,
    gath,
    loaded,
    sb,
    rb,
    send_sem,
    recv_sem,
):
    s = lax.axis_index("sector")
    r = lax.axis_index("radial")
    up = lax.rem(s + 1, secs)
    down = lax.rem(s + secs - 1, secs)

    loads = {
        name: pltpu.make_async_copy(src, dst, in_sem.at[i])
        for i, (name, src, dst) in enumerate(
            [
                ("sends", sends_hbm, sends),
                ("trace", trace_hbm, trace_map),
                *((t, fields_hbm.at[:, t], fields.at[t, pl.ds(0, COMP)]) for t in range(TILES)),
                ("operator", operator_hbm, operator),
                ("order", order_hbm, order),
                ("sizes", sizes_hbm, sizes),
                ("neighbours", neighbours_hbm, neighbours),
                ("pattern", pattern_hbm, pattern),
                ("heights", heights_hbm, tent_height),
                ("lift", lift_hbm, lift_map),
            ]
        )
    }
    urgent = ("sends", "trace", *range(TILES))
    for name in urgent:
        loads[name].start()

    rb[:, :, TRACE:TP] = jnp.zeros((LEVELS, 4, TP - TRACE, BND), F32)

    @pl.when(r == 0)
    def _():
        rb[:, 2] = jnp.zeros((LEVELS, TP, BND), F32)

    @pl.when(r == rads - 1)
    def _():
        rb[:, 3] = jnp.zeros((LEVELS, TP, BND), F32)

    barrier = pltpu.get_barrier_semaphore()

    def greet(a, b):
        pl.semaphore_signal(barrier, inc=1, device_id=(a, b), device_id_type=MESH)

    greet(up, r)
    greet(down, r)

    @pl.when(r > 0)
    def _():
        greet(s, r - 1)

    @pl.when(r < rads - 1)
    def _():
        greet(s, r + 1)

    for name in loads:
        if name not in urgent:
            loads[name].start()

    def copy(level, group, a, b):
        return pltpu.make_async_remote_copy(
            src_ref=sb.at[level, group, pl.ds(0, TRACE)],
            dst_ref=rb.at[level, group, pl.ds(0, TRACE)],
            send_sem=send_sem.at[level, group],
            recv_sem=recv_sem.at[level, group],
            device_id=(a, b),
            device_id_type=MESH,
        )

    def start(level):
        @pl.when(r < rads - 1)
        def _():
            copy(level, 2, s, r + 1).start()

        @pl.when(r > 0)
        def _():
            copy(level, 3, s, r - 1).start()

        copy(level, 0, up, r).start()
        copy(level, 1, down, r).start()

    def arrive(level):
        copy(level, 0, up, r).wait_recv()
        copy(level, 1, down, r).wait_recv()

        @pl.when(r > 0)
        def _():
            copy(level, 2, s, r - 1).wait_recv()

        @pl.when(r < rads - 1)
        def _():
            copy(level, 3, s, r + 1).wait_recv()

    def drain(level):
        copy(level, 0, up, r).wait_send()
        copy(level, 1, down, r).wait_send()

        @pl.when(r < rads - 1)
        def _():
            copy(level, 2, s, r + 1).wait_send()

        @pl.when(r > 0)
        def _():
            copy(level, 3, s, r - 1).wait_send()

    def fill_sends(level, got):
        for d in range(4):
            piece = got[:, BND * d : BND * d + BND]
            sb[level, d] = piece[:TP] + piece[TP:]

    tp[...] = jnp.zeros((TP, CP), F32)
    fields[:, COMP:CP] = jnp.zeros((TILES, CP - COMP, 128), F32)
    loads["sends"].wait()
    for m in range(ELEMS // KB):
        listed[KB * m : KB * m + KB] = one_hot(sends[...], KB * m)
    loads["trace"].wait()
    tp[0:TRACE, 0:COMP] = trace_map[...]
    t3[0:TP] = left3(tp[...])
    for t in range(TILES):
        loads[t].wait()
    hi, lo = hi_lo(jnp.concatenate([fields[t] for t in range(TILES)], axis=1))
    o = dot(t3[0:TP], jnp.concatenate([hi, hi, lo], axis=0))
    o = jnp.concatenate(hi_lo(o), axis=0)
    got = dot(o, listed[...])
    fill_sends(0, got)
    pl.semaphore_wait(
        barrier, 2 + jnp.where(r > 0, 1, 0) + jnp.where(r < rads - 1, 1, 0)
    )
    start(0)
    flow[...] = o
    rows[0:CP] = hi
    rows[CP : 2 * CP] = lo

    ap[...] = jnp.zeros((CP, CP), F32)
    lp[...] = jnp.zeros((FACES * TP, 256), F32)
    loads["operator"].wait()
    ap[0:COMP, 0:COMP] = operator[...]
    p1 = ap[...]
    a3[0:CP] = left3(p1)
    b1 = right3(p1)
    p2 = dot(a3[0:CP], b1)
    a3[CP : 2 * CP] = left3(p2)
    b2 = right3(p2)
    p34 = dot(a3[0 : 2 * CP], b2)
    a3[2 * CP : 4 * CP] = left3(p34)
    b4 = right3(p34[CP:])
    t3[TP : 2 * TP] = left3(dot(t3[0:TP], b1))
    t3[2 * TP : 4 * TP] = left3(dot(t3[0 : 2 * TP], b2))
    t3[4 * TP : 8 * TP] = left3(dot(t3[0 : 4 * TP], b4))
    t3[8 * TP : 9 * TP] = left3(dot(t3[4 * TP : 5 * TP], b4))

    for name in ("order", "sizes", "neighbours", "pattern", "heights"):
        loads[name].wait()
    line = lax.broadcasted_iota(I32, (16, 128), 0)
    lane = lax.broadcasted_iota(I32, (16, 128), 1)
    shift = jnp.zeros((16, 128), I32)
    limit = jnp.zeros((16, 128), I32)
    begin = jnp.int32(0)
    for l in range(LEVELS):
        size = sizes[l]
        mine = (line >= 3 * l) & (line < 3 * l + 3)
        shift = jnp.where(mine, begin - BLOCK * l, shift)
        limit = jnp.where(mine, BLOCK * l + size, limit)
        begin = begin + size
    slot = 128 * line + lane
    place = jnp.minimum(jnp.maximum(slot + shift, 0), ELEMS - 1)
    element = jnp.where(slot < limit, look_up(order[...], place), -1)
    tall = jnp.concatenate([element.astype(F32), jnp.zeros((112, 128), F32)], axis=0)
    tall = jnp.transpose(tall)
    for l in range(LEVELS):
        for t in range(3):
            n = 3 * l + t
            erow[l, :, 128 * t : 128 * t + 128] = element[n : n + 1]
            ecol[l, 128 * t : 128 * t + 128] = jnp.broadcast_to(tall[:, n : n + 1], (128, 128))
    line = lax.broadcasted_iota(I32, (8, ELEMS), 0)
    extra = jnp.where(line == 0, jnp.broadcast_to(pattern[...], (8, ELEMS)), 0)
    near = neighbours[...]
    numbers = jnp.concatenate([near >> 8, near & 255, extra], axis=0)
    rows[2 * CP :] = numbers.astype(F32).astype(BF16)
    loads["lift"].wait()
    for f in range(FACES):
        lp[TP * f : TP * f + TRACE, 0:COMP] = lift_map[:, f]
    l3[...] = left3(jnp.transpose(lp[...])[0:CP])

    def powers(l):
        h = height[l]
        ps = [jnp.ones_like(h)]
        for k in range(DEG):
            ps.append(ps[k] * h)
        return ps

    def finish(l):
        x = loaded[...]
        x3 = right3(x)
        hs = powers(l)
        y, v = x, x * COEF[HALF]
        for k in range(1, HALF + 1):
            u = dot(a3[CP * (k - 1) : CP * k], x3)
            if k < HALF:
                y += u * (hs[k] * COEF[k])
            v += u * (hs[k] * COEF[HALF + k])
        y += dot(a3[CP * (HALF - 1) :], right3(v * hs[HALF]))
        hl = jnp.concatenate(hi_lo(y), axis=0)
        for n in range(ELEMS // KB):
            here = slice(KB * n, KB * n + KB)
            got = dot(hl, scatter[:, here])
            got = got[:COMP] + got[CP : CP + COMP]
            for t in range(KB // 128):
                place = pl.ds(n * (KB // 128) + t, COMP, stride=8)
                if l == 0:
                    out[place] = got[:, 128 * t : 128 * t + 128]
                else:
                    out[place] += got[:, 128 * t : 128 * t + 128]

    for l in range(LEVELS):
        if l > 0:
            finish(l - 1)
            ones = jnp.ones((16, BLOCK), BF16)
            for n in range(ELEMS // KB):
                here = slice(KB * n, KB * n + KB)
                got = dot(jnp.concatenate([fresh[...], ones], axis=0), scatter[:, here])
                keep = jnp.broadcast_to(1.0 - got[2 * TP : 2 * TP + 1], (2 * TP, KB))
                flow[:, here] = (flow[:, here].astype(F32) * keep + got[: 2 * TP]).astype(BF16)

        moved = jnp.zeros((2 * CP + 16, BLOCK), F32)
        for m in range(ELEMS // KB):
            moved += dot(rows[:, KB * m : KB * m + KB], one_hot(erow[l], KB * m))
        start_x[...] = moved[:CP] + moved[CP : 2 * CP]
        numbers = moved[2 * CP :].astype(I32)
        near = numbers[0:4] * 256 + numbers[4:8]
        for f in range(FACES):
            nbx[:, BLOCK * f : BLOCK * f + BLOCK] = near[f : f + 1]
        kind = numbers[8:9]
        h = jnp.zeros((1, BLOCK), F32)
        for p in range(16):
            h = jnp.where(kind == p, tent_height[p], h)
        height[l] = h
        for f in range(0, FACES * BLOCK, 2 * KB):
            here = slice(f, f + 2 * KB)
            row = nbx[:, here]
            acc = jnp.zeros((2 * TP, 2 * KB), F32)
            for m in range(ELEMS // KB):
                acc += dot(flow[:, KB * m : KB * m + KB], one_hot(row, KB * m))
            gath[:, here] = acc
            for m in range(SLOTS // KB):
                catch[KB * m : KB * m + KB, here] = one_hot(row, ELEMS + KB * m)
        for t in range(ELEMS // 128):
            row = lax.broadcasted_iota(I32, (BLOCK, 128), 1).astype(F32) + 128.0 * t
            hit = jnp.where(ecol[l] == row, 1.0, 0.0).astype(BF16)
            scatter[:, 128 * t : 128 * t + 128] = hit
        if l < LEVELS - 1:
            got = dot(flow[...], listed[...])
            for d in range(4):
                row = sends[:, BND * d : BND * d + BND].astype(F32)
                hit = jnp.where(ecol[l] == jnp.broadcast_to(row, (BLOCK, BND)), 1.0, 0.0)
                pick[:, BND * d : BND * d + BND] = hit.astype(BF16)
            gone = dot(jnp.ones((16, BLOCK), BF16), pick[...])[0:1]
            part[...] = got * jnp.broadcast_to(1.0 - gone, (2 * TP, SLOTS))
        drain(l)
        arrive(l)
        come = jnp.concatenate([rb[l, d] for d in range(4)], axis=1)
        come = dot(jnp.concatenate(hi_lo(come), axis=0), catch[...])
        his, los = [], []
        for f in range(FACES):
            here = slice(BLOCK * f, BLOCK * f + BLOCK)
            acc = (gath[:, here] + come[:, here]).astype(BF16)
            his.append(acc[:TP])
            los.append(acc[TP:])
        x = start_x[...] + dot(l3[...], jnp.concatenate(his + his + los, axis=0))
        loaded[...] = x
        if l < LEVELS - 1:
            x3 = right3(x)
            hs = powers(l)
            o = dot(t3[0:TP], x3)
            for k in range(1, DEG + 1):
                o += dot(t3[TP * k : TP * k + TP], x3) * (hs[k] * COEF[k])
            o = jnp.concatenate(hi_lo(o), axis=0)
            fresh[...] = o
            fill_sends(l + 1, part[...] + dot(o, pick[...]))
            start(l + 1)

    finish(LEVELS - 1)

def solution(mesh):
    secs, rads = mesh.shape["sector"], mesh.shape["radial"]
    hbm = pl.BlockSpec(memory_space=pltpu.HBM)

    def body(
        fields,
        pattern,
        tent_order,
        level_sizes,
        send_rows,
        neighbours,
        operator,
        trace_map,
        lift_map,
        tent_height,
    ):
        args = (
            fields.reshape(COMP, TILES, 128),
            pattern[0],
            tent_order[0],
            level_sizes[0, 0],
            neighbours[0, 0],
            send_rows.reshape(1, SLOTS),
            operator,
            trace_map,
            jnp.transpose(lift_map, (2, 0, 1)),
            tent_height,
        )
        args = tuple(pltpu.with_memory_space_constraint(a, pltpu.HBM) for a in args)
        homes = [pltpu.VMEM((TILES, CP, 128), F32)] + [
            (pltpu.SMEM if len(a.shape) == 1 else pltpu.VMEM)(a.shape, a.dtype) for a in args[1:]
        ]
        out = pl.pallas_call(
            functools.partial(kernel, secs, rads),
            out_shape=jax.ShapeDtypeStruct((COMP * 8, 128), F32),
            in_specs=[hbm] * len(args),
            out_specs=pl.BlockSpec(memory_space=pltpu.VMEM),
            scratch_shapes=homes
            + [
                pltpu.SemaphoreType.DMA((TILES + len(args) - 1,)),
                pltpu.VMEM((TP, CP), F32),
                pltpu.VMEM((CP, CP), F32),
                pltpu.VMEM((FACES * TP, 256), F32),
                pltpu.VMEM(((DEG + 1) * TP, 3 * CP), BF16),
                pltpu.VMEM((HALF * CP, 3 * CP), BF16),
                pltpu.VMEM((CP, 3 * FACES * TP), BF16),
                pltpu.VMEM((2 * CP + 16, ELEMS), BF16),
                pltpu.VMEM((LEVELS, 1, BLOCK), I32),
                pltpu.VMEM((LEVELS, BLOCK, 128), F32),
                pltpu.VMEM((BLOCK, ELEMS), BF16),
                pltpu.VMEM((BLOCK, SLOTS), BF16),
                pltpu.VMEM((ELEMS, SLOTS), BF16),
                pltpu.VMEM((SLOTS, FACES * BLOCK), BF16),
                pltpu.VMEM((1, FACES * BLOCK), I32),
                pltpu.VMEM((LEVELS, 1, BLOCK), F32),
                pltpu.VMEM((CP, BLOCK), F32),
                pltpu.VMEM((2 * TP, ELEMS), BF16),
                pltpu.VMEM((2 * TP, BLOCK), BF16),
                pltpu.VMEM((2 * TP, SLOTS), F32),
                pltpu.VMEM((2 * TP, FACES * BLOCK), F32),
                pltpu.VMEM((CP, BLOCK), F32),
                pltpu.VMEM((LEVELS, 4, TP, BND), F32),
                pltpu.VMEM((LEVELS, 4, TP, BND), F32),
                pltpu.SemaphoreType.DMA((LEVELS, 4)),
                pltpu.SemaphoreType.DMA((LEVELS, 4)),
            ],
            compiler_params=pltpu.CompilerParams(
                collective_id=0, has_side_effects=True, vmem_limit_bytes=32 * 2**20
            ),
            name="tent_layer",
        )(*args)
        return out.reshape(1, 1, COMP, ELEMS)

    block = P("sector", "radial", None)
    wide = P("sector", "radial", None, None)
    return jax.shard_map(
        body,
        mesh=mesh,
        in_specs=(wide, block, block, block, wide, wide, P(), P(), P(), P()),
        out_specs=wide,
        check_vma=False,
    )
```

```python
import functools

import jax
import jax.numpy as jnp
import numpy as np
from jax import lax
from jax.experimental import pallas as pl
from jax.experimental.pallas import tpu as pltpu
from jax.sharding import PartitionSpec as P

LEVELS = 4
FACES = 4
SUBSTEPS = 2
TERMS = 4
BLOCK = 384
ELEMS = 1024
COMP = 140
TRACE = 60
BND = 128
CP = 144
TP = 64
SLOTS = 4 * BND
TILES = ELEMS // 128
KB = 256

MESH = pl.DeviceIdType.MESH
F32 = jnp.float32
BF16 = jnp.bfloat16
I32 = jnp.int32


def substep_powers():
    one = np.array([1.0 / np.prod(np.arange(1, k + 1)) for k in range(TERMS + 1)])
    total = np.array([1.0])
    for _ in range(SUBSTEPS):
        total = np.convolve(total, one)
    return [float(c) for c in total]


COEF = substep_powers()
DEG = SUBSTEPS * TERMS
HALF = DEG // 2


def hi_lo(x):
    hi = x.astype(BF16)
    return hi, (x - hi.astype(F32)).astype(BF16)


def right3(x):
    hi, lo = hi_lo(x)
    return jnp.concatenate([hi, hi, lo], axis=0)


def left3(m):
    hi, lo = hi_lo(m)
    return jnp.concatenate([hi, lo, hi], axis=1)


def dot(a, b):
    return jnp.dot(a, b, preferred_element_type=F32)


def one_hot(row, base):
    n = row.shape[1]
    line = lax.broadcasted_iota(I32, (KB, n), 0).astype(F32).astype(BF16)
    row = jnp.minimum(jnp.maximum(row - base, -1), KB).astype(F32).astype(BF16)
    return jnp.where(line == jnp.broadcast_to(row, (KB, n)), jnp.bfloat16(1), jnp.bfloat16(0))


def look_up(table, index):
    lane = index & 127
    tile = index >> 7
    out = jnp.zeros(index.shape, table.dtype)
    for m in range(table.shape[1] // 128):
        part = jnp.broadcast_to(table[:, 128 * m : 128 * m + 128], index.shape)
        got = jnp.take_along_axis(part, lane, axis=1, mode="promise_in_bounds")
        out = jnp.where(tile == m, got, out)
    return out


def kernel(
    secs,
    rads,
    fields_hbm,
    pattern_hbm,
    order_hbm,
    sizes_hbm,
    neighbours_hbm,
    sends_hbm,
    operator_hbm,
    trace_hbm,
    lift_hbm,
    heights_hbm,
    out,
    fields,
    pattern,
    order,
    sizes,
    neighbours,
    sends,
    operator,
    trace_map,
    lift_map,
    tent_height,
    in_sem,
    tp,
    ap,
    lp,
    t3,
    a3,
    l3,
    rows,
    erow,
    ecol,
    scatter,
    pick,
    listed,
    catch,
    nbx,
    height,
    start_x,
    flow,
    fresh,
    part,
    gath,
    loaded,
    sb,
    rb,
    send_sem,
    recv_sem,
):
    s = lax.axis_index("sector")
    r = lax.axis_index("radial")
    up = lax.rem(s + 1, secs)
    down = lax.rem(s + secs - 1, secs)

    loads = {
        name: pltpu.make_async_copy(src, dst, in_sem.at[i])
        for i, (name, src, dst) in enumerate(
            [
                ("sends", sends_hbm, sends),
                ("trace", trace_hbm, trace_map),
                ("fields", fields_hbm, fields),
                ("operator", operator_hbm, operator),
                ("order", order_hbm, order),
                ("sizes", sizes_hbm, sizes),
                ("neighbours", neighbours_hbm, neighbours),
                ("pattern", pattern_hbm, pattern),
                ("heights", heights_hbm, tent_height),
                ("lift", lift_hbm, lift_map),
            ]
        )
    }
    urgent = ("fields", "sends", "trace")
    for name in urgent:
        loads[name].start()

    rb[:, :, TRACE:TP] = jnp.zeros((LEVELS, 4, TP - TRACE, BND), F32)

    @pl.when(r == 0)
    def _():
        rb[:, 2] = jnp.zeros((LEVELS, TP, BND), F32)

    @pl.when(r == rads - 1)
    def _():
        rb[:, 3] = jnp.zeros((LEVELS, TP, BND), F32)

    barrier = pltpu.get_barrier_semaphore()

    def greet(a, b):
        pl.semaphore_signal(barrier, inc=1, device_id=(a, b), device_id_type=MESH)

    greet(up, r)
    greet(down, r)

    @pl.when(r > 0)
    def _():
        greet(s, r - 1)

    @pl.when(r < rads - 1)
    def _():
        greet(s, r + 1)

    for name in loads:
        if name not in urgent:
            loads[name].start()

    def copy(level, group, a, b):
        return pltpu.make_async_remote_copy(
            src_ref=sb.at[level, group, pl.ds(0, TRACE)],
            dst_ref=rb.at[level, group, pl.ds(0, TRACE)],
            send_sem=send_sem.at[level % 2, group],
            recv_sem=recv_sem.at[level % 2, group],
            device_id=(a, b),
            device_id_type=MESH,
        )

    def start(level):
        @pl.when(r < rads - 1)
        def _():
            copy(level, 2, s, r + 1).start()

        @pl.when(r > 0)
        def _():
            copy(level, 3, s, r - 1).start()

        copy(level, 0, up, r).start()
        copy(level, 1, down, r).start()

    def arrive(level):
        copy(level, 0, up, r).wait_recv()
        copy(level, 1, down, r).wait_recv()

        @pl.when(r > 0)
        def _():
            copy(level, 2, s, r - 1).wait_recv()

        @pl.when(r < rads - 1)
        def _():
            copy(level, 3, s, r + 1).wait_recv()

    def drain(level):
        copy(level, 0, up, r).wait_send()
        copy(level, 1, down, r).wait_send()

        @pl.when(r < rads - 1)
        def _():
            copy(level, 2, s, r + 1).wait_send()

        @pl.when(r > 0)
        def _():
            copy(level, 3, s, r - 1).wait_send()

    def fill_sends(level, got):
        for d in range(4):
            piece = got[:, BND * d : BND * d + BND]
            sb[level, d] = piece[:TP] + piece[TP:]

    tp[...] = jnp.zeros((TP, CP), F32)
    loads["sends"].wait()
    for m in range(ELEMS // KB):
        listed[KB * m : KB * m + KB] = one_hot(sends[...], KB * m)
    loads["trace"].wait()
    tp[0:TRACE, 0:COMP] = trace_map[...]
    t3[0:TP] = left3(tp[...])
    loads["fields"].wait()
    piece = [fields[pl.ds(t, COMP, stride=TILES)] for t in range(TILES)]
    piece = jnp.concatenate(piece, axis=1)
    piece = jnp.concatenate([piece, jnp.zeros((CP - COMP, ELEMS), F32)], axis=0)
    hi, lo = hi_lo(piece)
    o = dot(t3[0:TP], jnp.concatenate([hi, hi, lo], axis=0))
    o = jnp.concatenate(hi_lo(o), axis=0)
    got = dot(o, listed[...])
    fill_sends(0, got)
    pl.semaphore_wait(
        barrier, 2 + jnp.where(r > 0, 1, 0) + jnp.where(r < rads - 1, 1, 0)
    )
    start(0)
    flow[...] = o
    rows[0:CP] = hi
    rows[CP : 2 * CP] = lo

    ap[...] = jnp.zeros((CP, CP), F32)
    lp[...] = jnp.zeros((FACES * TP, 256), F32)
    loads["operator"].wait()
    ap[0:COMP, 0:COMP] = operator[...]
    p1 = ap[...]
    a3[0:CP] = left3(p1)
    b1 = right3(p1)
    p2 = dot(a3[0:CP], b1)
    a3[CP : 2 * CP] = left3(p2)
    b2 = right3(p2)
    p34 = dot(a3[0 : 2 * CP], b2)
    a3[2 * CP : 4 * CP] = left3(p34)
    b4 = right3(p34[CP:])
    t3[TP : 2 * TP] = left3(dot(t3[0:TP], b1))
    t3[2 * TP : 4 * TP] = left3(dot(t3[0 : 2 * TP], b2))
    t3[4 * TP : 8 * TP] = left3(dot(t3[0 : 4 * TP], b4))
    t3[8 * TP : 9 * TP] = left3(dot(t3[4 * TP : 5 * TP], b4))

    for name in ("order", "sizes", "neighbours", "pattern", "heights"):
        loads[name].wait()
    line = lax.broadcasted_iota(I32, (16, 128), 0)
    lane = lax.broadcasted_iota(I32, (16, 128), 1)
    shift = jnp.zeros((16, 128), I32)
    limit = jnp.zeros((16, 128), I32)
    begin = jnp.int32(0)
    for l in range(LEVELS):
        size = sizes[l]
        mine = (line >= 3 * l) & (line < 3 * l + 3)
        shift = jnp.where(mine, begin - BLOCK * l, shift)
        limit = jnp.where(mine, BLOCK * l + size, limit)
        begin = begin + size
    slot = 128 * line + lane
    place = jnp.minimum(jnp.maximum(slot + shift, 0), ELEMS - 1)
    element = jnp.where(slot < limit, look_up(order[...], place), -1)
    tall = jnp.concatenate([element.astype(F32), jnp.zeros((112, 128), F32)], axis=0)
    tall = jnp.transpose(tall)
    for l in range(LEVELS):
        for t in range(3):
            n = 3 * l + t
            erow[l, :, 128 * t : 128 * t + 128] = element[n : n + 1]
            ecol[l, 128 * t : 128 * t + 128] = jnp.broadcast_to(tall[:, n : n + 1], (128, 128))
    line = lax.broadcasted_iota(I32, (8, ELEMS), 0)
    extra = jnp.where(line == 0, jnp.broadcast_to(pattern[...], (8, ELEMS)), 0)
    near = neighbours[...]
    numbers = jnp.concatenate([near >> 8, near & 255, extra], axis=0)
    rows[2 * CP :] = numbers.astype(F32).astype(BF16)
    loads["lift"].wait()
    for f in range(FACES):
        lp[TP * f : TP * f + TRACE, 0:COMP] = lift_map[:, f]
    l3[...] = left3(jnp.transpose(lp[...])[0:CP])

    def powers(l):
        h = height[l]
        ps = [jnp.ones_like(h)]
        for k in range(DEG):
            ps.append(ps[k] * h)
        return ps

    def finish(l):
        x = loaded[...]
        x3 = right3(x)
        hs = powers(l)
        y, v = x, x * COEF[HALF]
        for k in range(1, HALF + 1):
            u = dot(a3[CP * (k - 1) : CP * k], x3)
            if k < HALF:
                y += u * (hs[k] * COEF[k])
            v += u * (hs[k] * COEF[HALF + k])
        y += dot(a3[CP * (HALF - 1) :], right3(v * hs[HALF]))
        hl = jnp.concatenate(hi_lo(y), axis=0)
        for n in range(ELEMS // KB):
            here = slice(KB * n, KB * n + KB)
            got = dot(hl, scatter[:, here])
            got = got[:COMP] + got[CP : CP + COMP]
            for t in range(KB // 128):
                place = pl.ds(n * (KB // 128) + t, COMP, stride=8)
                if l == 0:
                    out[place] = got[:, 128 * t : 128 * t + 128]
                else:
                    out[place] += got[:, 128 * t : 128 * t + 128]

    for l in range(LEVELS):
        if l > 0:
            finish(l - 1)
            ones = jnp.ones((16, BLOCK), BF16)
            for n in range(ELEMS // KB):
                here = slice(KB * n, KB * n + KB)
                got = dot(jnp.concatenate([fresh[...], ones], axis=0), scatter[:, here])
                keep = jnp.broadcast_to(1.0 - got[2 * TP : 2 * TP + 1], (2 * TP, KB))
                flow[:, here] = (flow[:, here].astype(F32) * keep + got[: 2 * TP]).astype(BF16)

        moved = jnp.zeros((2 * CP + 16, BLOCK), F32)
        for m in range(ELEMS // KB):
            moved += dot(rows[:, KB * m : KB * m + KB], one_hot(erow[l], KB * m))
        start_x[...] = moved[:CP] + moved[CP : 2 * CP]
        numbers = moved[2 * CP :].astype(I32)
        near = numbers[0:4] * 256 + numbers[4:8]
        for f in range(FACES):
            nbx[:, BLOCK * f : BLOCK * f + BLOCK] = near[f : f + 1]
        kind = numbers[8:9]
        h = jnp.zeros((1, BLOCK), F32)
        for p in range(16):
            h = jnp.where(kind == p, tent_height[p], h)
        height[l] = h
        for f in range(0, FACES * BLOCK, 2 * KB):
            here = slice(f, f + 2 * KB)
            row = nbx[:, here]
            acc = jnp.zeros((2 * TP, 2 * KB), F32)
            for m in range(ELEMS // KB):
                acc += dot(flow[:, KB * m : KB * m + KB], one_hot(row, KB * m))
            gath[:, here] = acc
            for m in range(SLOTS // KB):
                catch[KB * m : KB * m + KB, here] = one_hot(row, ELEMS + KB * m)
        for t in range(ELEMS // 128):
            row = lax.broadcasted_iota(I32, (BLOCK, 128), 1).astype(F32) + 128.0 * t
            hit = jnp.where(ecol[l] == row, 1.0, 0.0).astype(BF16)
            scatter[:, 128 * t : 128 * t + 128] = hit
        if l < LEVELS - 1:
            got = dot(flow[...], listed[...])
            for d in range(4):
                row = sends[:, BND * d : BND * d + BND].astype(F32)
                hit = jnp.where(ecol[l] == jnp.broadcast_to(row, (BLOCK, BND)), 1.0, 0.0)
                pick[:, BND * d : BND * d + BND] = hit.astype(BF16)
            gone = dot(jnp.ones((16, BLOCK), BF16), pick[...])[0:1]
            part[...] = got * jnp.broadcast_to(1.0 - gone, (2 * TP, SLOTS))
        drain(l)
        arrive(l)
        come = jnp.concatenate([rb[l, d] for d in range(4)], axis=1)
        come = dot(jnp.concatenate(hi_lo(come), axis=0), catch[...])
        his, los = [], []
        for f in range(FACES):
            here = slice(BLOCK * f, BLOCK * f + BLOCK)
            acc = (gath[:, here] + come[:, here]).astype(BF16)
            his.append(acc[:TP])
            los.append(acc[TP:])
        x = start_x[...] + dot(l3[...], jnp.concatenate(his + his + los, axis=0))
        loaded[...] = x
        if l < LEVELS - 1:
            x3 = right3(x)
            hs = powers(l)
            o = dot(t3[0:TP], x3)
            for k in range(1, DEG + 1):
                o += dot(t3[TP * k : TP * k + TP], x3) * (hs[k] * COEF[k])
            o = jnp.concatenate(hi_lo(o), axis=0)
            fresh[...] = o
            fill_sends(l + 1, part[...] + dot(o, pick[...]))
            start(l + 1)

    finish(LEVELS - 1)

def solution(mesh):
    secs, rads = mesh.shape["sector"], mesh.shape["radial"]
    hbm = pl.BlockSpec(memory_space=pltpu.HBM)

    def body(
        fields,
        pattern,
        tent_order,
        level_sizes,
        send_rows,
        neighbours,
        operator,
        trace_map,
        lift_map,
        tent_height,
    ):
        args = (
            fields.reshape(COMP * TILES, 128),
            pattern[0],
            tent_order[0],
            level_sizes[0, 0],
            neighbours[0, 0],
            send_rows.reshape(1, SLOTS),
            operator,
            trace_map,
            jnp.transpose(lift_map, (2, 0, 1)),
            tent_height,
        )
        args = tuple(pltpu.with_memory_space_constraint(a, pltpu.HBM) for a in args)
        homes = [
            (pltpu.SMEM if len(a.shape) == 1 else pltpu.VMEM)(a.shape, a.dtype) for a in args
        ]
        out = pl.pallas_call(
            functools.partial(kernel, secs, rads),
            out_shape=jax.ShapeDtypeStruct((COMP * 8, 128), F32),
            in_specs=[hbm] * len(args),
            out_specs=pl.BlockSpec(memory_space=pltpu.VMEM),
            scratch_shapes=homes
            + [
                pltpu.SemaphoreType.DMA((len(args),)),
                pltpu.VMEM((TP, CP), F32),
                pltpu.VMEM((CP, CP), F32),
                pltpu.VMEM((FACES * TP, 256), F32),
                pltpu.VMEM(((DEG + 1) * TP, 3 * CP), BF16),
                pltpu.VMEM((HALF * CP, 3 * CP), BF16),
                pltpu.VMEM((CP, 3 * FACES * TP), BF16),
                pltpu.VMEM((2 * CP + 16, ELEMS), BF16),
                pltpu.VMEM((LEVELS, 1, BLOCK), I32),
                pltpu.VMEM((LEVELS, BLOCK, 128), F32),
                pltpu.VMEM((BLOCK, ELEMS), BF16),
                pltpu.VMEM((BLOCK, SLOTS), BF16),
                pltpu.VMEM((ELEMS, SLOTS), BF16),
                pltpu.VMEM((SLOTS, FACES * BLOCK), BF16),
                pltpu.VMEM((1, FACES * BLOCK), I32),
                pltpu.VMEM((LEVELS, 1, BLOCK), F32),
                pltpu.VMEM((CP, BLOCK), F32),
                pltpu.VMEM((2 * TP, ELEMS), BF16),
                pltpu.VMEM((2 * TP, BLOCK), BF16),
                pltpu.VMEM((2 * TP, SLOTS), F32),
                pltpu.VMEM((2 * TP, FACES * BLOCK), F32),
                pltpu.VMEM((CP, BLOCK), F32),
                pltpu.VMEM((LEVELS, 4, TP, BND), F32),
                pltpu.VMEM((LEVELS, 4, TP, BND), F32),
                pltpu.SemaphoreType.DMA((2, 4)),
                pltpu.SemaphoreType.DMA((2, 4)),
            ],
            compiler_params=pltpu.CompilerParams(
                collective_id=0, has_side_effects=True, vmem_limit_bytes=32 * 2**20
            ),
            name="tent_layer",
        )(*args)
        return out.reshape(1, 1, COMP, ELEMS)

    block = P("sector", "radial", None)
    wide = P("sector", "radial", None, None)
    return jax.shard_map(
        body,
        mesh=mesh,
        in_specs=(wide, block, block, block, wide, wide, P(), P(), P(), P()),
        out_specs=wide,
        check_vma=False,
    )
```

```python
import functools

import jax
import jax.numpy as jnp
import numpy as np
from jax import lax
from jax.experimental import pallas as pl
from jax.experimental.pallas import tpu as pltpu
from jax.sharding import PartitionSpec as P

LEVELS = 4
FACES = 4
SUBSTEPS = 2
TERMS = 4
BLOCK = 384
ELEMS = 1024
COMP = 140
TRACE = 60
BND = 128
CP = 144
TP = 64
SLOTS = 4 * BND
TILES = ELEMS // 128
KB = 256

MESH = pl.DeviceIdType.MESH
F32 = jnp.float32
BF16 = jnp.bfloat16
I32 = jnp.int32


def substep_powers():
    one = np.array([1.0 / np.prod(np.arange(1, k + 1)) for k in range(TERMS + 1)])
    total = np.array([1.0])
    for _ in range(SUBSTEPS):
        total = np.convolve(total, one)
    return [float(c) for c in total]


COEF = substep_powers()
DEG = SUBSTEPS * TERMS
HALF = DEG // 2


def hi_lo(x):
    hi = x.astype(BF16)
    return hi, (x - hi.astype(F32)).astype(BF16)


def right3(x):
    hi, lo = hi_lo(x)
    return jnp.concatenate([hi, hi, lo], axis=0)


def left3(m):
    hi, lo = hi_lo(m)
    return jnp.concatenate([hi, lo, hi], axis=1)


def dot(a, b):
    return jnp.dot(a, b, preferred_element_type=F32)


def one_hot(row, base):
    n = row.shape[1]
    line = lax.broadcasted_iota(I32, (KB, n), 0).astype(F32).astype(BF16)
    row = jnp.minimum(jnp.maximum(row - base, -1), KB).astype(F32).astype(BF16)
    return jnp.where(line == jnp.broadcast_to(row, (KB, n)), jnp.bfloat16(1), jnp.bfloat16(0))


def look_up(table, index):
    lane = index & 127
    tile = index >> 7
    out = jnp.zeros(index.shape, table.dtype)
    for m in range(table.shape[1] // 128):
        part = jnp.broadcast_to(table[:, 128 * m : 128 * m + 128], index.shape)
        got = jnp.take_along_axis(part, lane, axis=1, mode="promise_in_bounds")
        out = jnp.where(tile == m, got, out)
    return out


def kernel(
    secs,
    rads,
    fields_hbm,
    pattern_hbm,
    order_hbm,
    sizes_hbm,
    neighbours_hbm,
    sends_hbm,
    operator_hbm,
    trace_hbm,
    lift_hbm,
    heights_hbm,
    out,
    fields,
    pattern,
    order,
    sizes,
    neighbours,
    sends,
    operator,
    trace_map,
    lift_map,
    tent_height,
    in_sem,
    tp,
    ap,
    lp,
    t3,
    a3,
    l3,
    rows,
    erow,
    ehi,
    elo,
    scatter,
    ends,
    pick,
    listed,
    catch,
    nbx,
    height,
    flow,
    fresh,
    part,
    gath,
    loaded,
    sb,
    rb,
    send_sem,
    recv_sem,
):
    s = lax.axis_index("sector")
    r = lax.axis_index("radial")
    up = lax.rem(s + 1, secs)
    down = lax.rem(s + secs - 1, secs)

    loads = {
        name: pltpu.make_async_copy(src, dst, in_sem.at[i])
        for i, (name, src, dst) in enumerate(
            [
                ("sends", sends_hbm, sends),
                ("trace", trace_hbm, trace_map),
                ("fields", fields_hbm, fields),
                ("operator", operator_hbm, operator),
                ("order", order_hbm, order),
                ("sizes", sizes_hbm, sizes),
                ("neighbours", neighbours_hbm, neighbours),
                ("pattern", pattern_hbm, pattern),
                ("heights", heights_hbm, tent_height),
                ("lift", lift_hbm, lift_map),
            ]
        )
    }
    urgent = ("fields", "sends", "trace")
    for name in urgent:
        loads[name].start()

    rb[:, :, TRACE:TP] = jnp.zeros((LEVELS, 4, TP - TRACE, BND), F32)

    @pl.when(r == 0)
    def _():
        rb[:, 2] = jnp.zeros((LEVELS, TP, BND), F32)

    @pl.when(r == rads - 1)
    def _():
        rb[:, 3] = jnp.zeros((LEVELS, TP, BND), F32)

    barrier = pltpu.get_barrier_semaphore()

    def greet(a, b):
        pl.semaphore_signal(barrier, inc=1, device_id=(a, b), device_id_type=MESH)

    greet(up, r)
    greet(down, r)

    @pl.when(r > 0)
    def _():
        greet(s, r - 1)

    @pl.when(r < rads - 1)
    def _():
        greet(s, r + 1)

    for name in loads:
        if name not in urgent:
            loads[name].start()

    def copy(level, group, a, b):
        return pltpu.make_async_remote_copy(
            src_ref=sb.at[level, group, pl.ds(0, TRACE)],
            dst_ref=rb.at[level, group, pl.ds(0, TRACE)],
            send_sem=send_sem.at[level % 2, group],
            recv_sem=recv_sem.at[level % 2, group],
            device_id=(a, b),
            device_id_type=MESH,
        )

    def start(level):
        @pl.when(r < rads - 1)
        def _():
            copy(level, 2, s, r + 1).start()

        @pl.when(r > 0)
        def _():
            copy(level, 3, s, r - 1).start()

        copy(level, 0, up, r).start()
        copy(level, 1, down, r).start()

    def arrive(level):
        copy(level, 0, up, r).wait_recv()
        copy(level, 1, down, r).wait_recv()

        @pl.when(r > 0)
        def _():
            copy(level, 2, s, r - 1).wait_recv()

        @pl.when(r < rads - 1)
        def _():
            copy(level, 3, s, r + 1).wait_recv()

    def drain(level):
        copy(level, 0, up, r).wait_send()
        copy(level, 1, down, r).wait_send()

        @pl.when(r < rads - 1)
        def _():
            copy(level, 2, s, r + 1).wait_send()

        @pl.when(r > 0)
        def _():
            copy(level, 3, s, r - 1).wait_send()

    def fill_sends(level, got):
        for d in range(4):
            piece = got[:, BND * d : BND * d + BND]
            sb[level, d] = piece[:TP] + piece[TP:]

    tp[...] = jnp.zeros((TP, CP), F32)
    loads["sends"].wait()
    for m in range(ELEMS // KB):
        listed[KB * m : KB * m + KB] = one_hot(sends[...], KB * m)
    loads["trace"].wait()
    tp[0:TRACE, 0:COMP] = trace_map[...]
    t3[0:TP] = left3(tp[...])
    loads["fields"].wait()
    piece = [fields[pl.ds(t, COMP, stride=TILES)] for t in range(TILES)]
    piece = jnp.concatenate(piece, axis=1)
    piece = jnp.concatenate([piece, jnp.zeros((CP - COMP, ELEMS), F32)], axis=0)
    hi, lo = hi_lo(piece)
    o = dot(t3[0:TP], jnp.concatenate([hi, hi, lo], axis=0))
    o = jnp.concatenate(hi_lo(o), axis=0)
    got = dot(o, listed[...])
    fill_sends(0, got)
    pl.semaphore_wait(
        barrier, 2 + jnp.where(r > 0, 1, 0) + jnp.where(r < rads - 1, 1, 0)
    )
    start(0)
    flow[...] = o
    rows[0:CP] = hi
    rows[CP : 2 * CP] = lo

    ap[...] = jnp.zeros((CP, CP), F32)
    lp[...] = jnp.zeros((FACES * TP, 256), F32)
    loads["operator"].wait()
    ap[0:COMP, 0:COMP] = operator[...]
    p1 = ap[...]
    a3[0:CP] = left3(p1)
    b1 = right3(p1)
    p2 = dot(a3[0:CP], b1)
    a3[CP : 2 * CP] = left3(p2)
    b2 = right3(p2)
    p34 = dot(a3[0 : 2 * CP], b2)
    a3[2 * CP : 4 * CP] = left3(p34)
    b4 = right3(p34[CP:])
    t3[TP : 2 * TP] = left3(dot(t3[0:TP], b1))
    t3[2 * TP : 4 * TP] = left3(dot(t3[0 : 2 * TP], b2))
    t3[4 * TP : 8 * TP] = left3(dot(t3[0 : 4 * TP], b4))
    t3[8 * TP : 9 * TP] = left3(dot(t3[4 * TP : 5 * TP], b4))

    for name in ("order", "sizes", "neighbours", "pattern", "heights"):
        loads[name].wait()
    line = lax.broadcasted_iota(I32, (16, 128), 0)
    lane = lax.broadcasted_iota(I32, (16, 128), 1)
    shift = jnp.zeros((16, 128), I32)
    limit = jnp.zeros((16, 128), I32)
    begin = jnp.int32(0)
    for l in range(LEVELS):
        size = sizes[l]
        mine = (line >= 3 * l) & (line < 3 * l + 3)
        shift = jnp.where(mine, begin - BLOCK * l, shift)
        limit = jnp.where(mine, BLOCK * l + size, limit)
        begin = begin + size
    slot = 128 * line + lane
    place = jnp.minimum(jnp.maximum(slot + shift, 0), ELEMS - 1)
    element = jnp.where(slot < limit, look_up(order[...], place), -1)
    tall = jnp.concatenate([element >> 7, element & 127, jnp.zeros((96, 128), I32)], axis=0).astype(F32)
    tall = jnp.transpose(tall)
    for l in range(LEVELS):
        for t in range(3):
            n = 3 * l + t
            erow[l, :, 128 * t : 128 * t + 128] = element[n : n + 1]
            here = slice(128 * t, 128 * t + 128)
            ehi[l, here] = jnp.broadcast_to(tall[:, n : n + 1], (128, 128)).astype(BF16)
            elo[l, here] = jnp.broadcast_to(tall[:, n + 16 : n + 17], (128, 128)).astype(BF16)
    line = lax.broadcasted_iota(I32, (8, ELEMS), 0)
    extra = jnp.where(line == 0, jnp.broadcast_to(pattern[...], (8, ELEMS)), 0)
    near = neighbours[...]
    numbers = jnp.concatenate([near >> 8, near & 255, extra], axis=0)
    rows[2 * CP :] = numbers.astype(F32).astype(BF16)
    loads["lift"].wait()
    for f in range(FACES):
        lp[TP * f : TP * f + TRACE, 0:COMP] = lift_map[:, f]
    l3[...] = left3(jnp.transpose(lp[...])[0:CP])

    def powers(l):
        h = height[l]
        ps = [jnp.ones_like(h)]
        for k in range(DEG):
            ps.append(ps[k] * h)
        return ps

    def by_face(got):
        his = [got[:TP, BLOCK * f : BLOCK * f + BLOCK] for f in range(FACES)]
        los = [got[TP:, BLOCK * f : BLOCK * f + BLOCK] for f in range(FACES)]
        return jnp.concatenate(his + his + los, axis=0)

    def traces(os, hs):
        o = os[0:TP]
        for k in range(1, DEG + 1):
            o += os[TP * k : TP * k + TP] * (hs[k] * COEF[k])
        return o

    def finish(l):
        x = loaded[...]
        x3 = right3(x)
        hs = powers(l)
        y, v = x, x * COEF[HALF]
        for k in range(1, HALF + 1):
            u = dot(a3[CP * (k - 1) : CP * k], x3)
            if k < HALF:
                y += u * (hs[k] * COEF[k])
            v += u * (hs[k] * COEF[HALF + k])
        y += dot(a3[CP * (HALF - 1) :], right3(v * hs[HALF]))
        ends[:, BLOCK * l : BLOCK * l + BLOCK] = jnp.concatenate(hi_lo(y), axis=0)

    def put(first, last, add):
        here = slice(BLOCK * first, BLOCK * last)
        for n in range(ELEMS // KB):
            got = dot(ends[:, here], scatter[here, KB * n : KB * n + KB])
            got = got[:COMP] + got[CP : CP + COMP]
            for t in range(KB // 128):
                place = pl.ds(n * (KB // 128) + t, COMP, stride=TILES)
                piece = got[:, 128 * t : 128 * t + 128]
                out[place] = out[place] + piece if add else piece

    for l in range(LEVELS):
        if l > 0:
            finish(l - 1)
            ones = jnp.ones((16, BLOCK), BF16)
            for n in range(ELEMS // KB):
                here = slice(KB * n, KB * n + KB)
                back = scatter[BLOCK * (l - 1) : BLOCK * l, here]
                got = dot(jnp.concatenate([fresh[...], ones], axis=0), back)
                keep = jnp.broadcast_to(1.0 - got[2 * TP : 2 * TP + 1], (2 * TP, KB))
                flow[:, here] = (flow[:, here].astype(F32) * keep + got[: 2 * TP]).astype(BF16)

        moved = jnp.zeros((2 * CP + 16, BLOCK), F32)
        for m in range(ELEMS // KB):
            moved += dot(rows[:, KB * m : KB * m + KB], one_hot(erow[l], KB * m))
        loaded[...] = moved[:CP] + moved[CP : 2 * CP]
        numbers = moved[2 * CP :].astype(I32)
        near = numbers[0:4] * 256 + numbers[4:8]
        for f in range(FACES):
            nbx[:, BLOCK * f : BLOCK * f + BLOCK] = near[f : f + 1]
        kind = numbers[8:9]
        h = jnp.zeros((1, BLOCK), F32)
        for p in range(16):
            h = jnp.where(kind == p, tent_height[p], h)
        height[l] = h
        for f in range(0, FACES * BLOCK, 2 * KB):
            here = slice(f, f + 2 * KB)
            row = nbx[:, here]
            acc = jnp.zeros((2 * TP, 2 * KB), F32)
            for m in range(ELEMS // KB):
                acc += dot(flow[:, KB * m : KB * m + KB], one_hot(row, KB * m))
            gath[:, here] = acc.astype(BF16)
            for m in range(SLOTS // KB):
                catch[KB * m : KB * m + KB, here] = one_hot(row, ELEMS + KB * m)
        loaded[...] += dot(l3[...], by_face(gath[...]))
        one, none = jnp.bfloat16(1), jnp.bfloat16(0)
        lane = lax.broadcasted_iota(I32, (BLOCK, 128), 1).astype(F32).astype(BF16)
        same = jnp.where(elo[l] == lane, one, none)
        for t in range(TILES):
            hit = jnp.where(ehi[l] == jnp.bfloat16(t), same, none)
            scatter[BLOCK * l : BLOCK * l + BLOCK, 128 * t : 128 * t + 128] = hit
        if l < LEVELS - 1:
            got = dot(flow[...], listed[...])
            for d in range(4):
                row = sends[:, BND * d : BND * d + BND]
                row = [
                    jnp.broadcast_to(digit.astype(F32).astype(BF16), (BLOCK, BND))
                    for digit in (row >> 7, row & 127)
                ]
                hit = jnp.where(elo[l] == row[1], one, none)
                pick[:, BND * d : BND * d + BND] = jnp.where(ehi[l] == row[0], hit, none)
            gone = dot(jnp.ones((16, BLOCK), BF16), pick[...])[0:1]
            part[...] = got * jnp.broadcast_to(1.0 - gone, (2 * TP, SLOTS))
        if l == LEVELS - 1:
            put(0, l, False)
        drain(l)
        arrive(l)
        got = jnp.concatenate([rb[l, d] for d in range(4)], axis=1)
        got = dot(jnp.concatenate(hi_lo(got), axis=0), catch[...]).astype(BF16)
        x = loaded[...] + dot(l3[...], by_face(got))
        loaded[...] = x
        if l < LEVELS - 1:
            o = traces(dot(t3[...], right3(x)), powers(l))
            o = jnp.concatenate(hi_lo(o), axis=0)
            fresh[...] = o
            fill_sends(l + 1, part[...] + dot(o, pick[...]))
            start(l + 1)

    finish(LEVELS - 1)
    put(LEVELS - 1, LEVELS, True)

def solution(mesh):
    secs, rads = mesh.shape["sector"], mesh.shape["radial"]
    hbm = pl.BlockSpec(memory_space=pltpu.HBM)

    def body(
        fields,
        pattern,
        tent_order,
        level_sizes,
        send_rows,
        neighbours,
        operator,
        trace_map,
        lift_map,
        tent_height,
    ):
        args = (
            fields.reshape(COMP * TILES, 128),
            pattern[0],
            tent_order[0],
            level_sizes[0, 0],
            neighbours[0, 0],
            send_rows.reshape(1, SLOTS),
            operator,
            trace_map,
            jnp.transpose(lift_map, (2, 0, 1)),
            tent_height,
        )
        args = tuple(pltpu.with_memory_space_constraint(a, pltpu.HBM) for a in args)
        homes = [
            (pltpu.SMEM if len(a.shape) == 1 else pltpu.VMEM)(a.shape, a.dtype) for a in args
        ]
        out = pl.pallas_call(
            functools.partial(kernel, secs, rads),
            out_shape=jax.ShapeDtypeStruct((COMP * 8, 128), F32),
            in_specs=[hbm] * len(args),
            out_specs=pl.BlockSpec(memory_space=pltpu.VMEM),
            scratch_shapes=homes
            + [
                pltpu.SemaphoreType.DMA((len(args),)),
                pltpu.VMEM((TP, CP), F32),
                pltpu.VMEM((CP, CP), F32),
                pltpu.VMEM((FACES * TP, 256), F32),
                pltpu.VMEM(((DEG + 1) * TP, 3 * CP), BF16),
                pltpu.VMEM((HALF * CP, 3 * CP), BF16),
                pltpu.VMEM((CP, 3 * FACES * TP), BF16),
                pltpu.VMEM((2 * CP + 16, ELEMS), BF16),
                pltpu.VMEM((LEVELS, 1, BLOCK), I32),
                pltpu.VMEM((LEVELS, BLOCK, 128), BF16),
                pltpu.VMEM((LEVELS, BLOCK, 128), BF16),
                pltpu.VMEM((LEVELS * BLOCK, ELEMS), BF16),
                pltpu.VMEM((2 * CP, LEVELS * BLOCK), BF16),
                pltpu.VMEM((BLOCK, SLOTS), BF16),
                pltpu.VMEM((ELEMS, SLOTS), BF16),
                pltpu.VMEM((SLOTS, FACES * BLOCK), BF16),
                pltpu.VMEM((1, FACES * BLOCK), I32),
                pltpu.VMEM((LEVELS, 1, BLOCK), F32),
                pltpu.VMEM((2 * TP, ELEMS), BF16),
                pltpu.VMEM((2 * TP, BLOCK), BF16),
                pltpu.VMEM((2 * TP, SLOTS), F32),
                pltpu.VMEM((2 * TP, FACES * BLOCK), BF16),
                pltpu.VMEM((CP, BLOCK), F32),
                pltpu.VMEM((LEVELS, 4, TP, BND), F32),
                pltpu.VMEM((LEVELS, 4, TP, BND), F32),
                pltpu.SemaphoreType.DMA((2, 4)),
                pltpu.SemaphoreType.DMA((2, 4)),
            ],
            compiler_params=pltpu.CompilerParams(
                collective_id=0, has_side_effects=True, vmem_limit_bytes=32 * 2**20
            ),
            name="tent_layer",
        )(*args)
        return out.reshape(1, 1, COMP, ELEMS)

    block = P("sector", "radial", None)
    wide = P("sector", "radial", None, None)
    return jax.shard_map(
        body,
        mesh=mesh,
        in_specs=(wide, block, block, block, wide, wide, P(), P(), P(), P()),
        out_specs=wide,
        check_vma=False,
    )
```

```python
import functools

import jax
import jax.numpy as jnp
import numpy as np
from jax import lax
from jax.experimental import pallas as pl
from jax.experimental.pallas import tpu as pltpu
from jax.sharding import PartitionSpec as P

LEVELS = 4
FACES = 4
SUBSTEPS = 2
TERMS = 4
BLOCK = 384
ELEMS = 1024
COMP = 140
TRACE = 60
BND = 128
CP = 144
TP = 64
SLOTS = 4 * BND
TILES = ELEMS // 128
KB = 256

MESH = pl.DeviceIdType.MESH
F32 = jnp.float32
BF16 = jnp.bfloat16
I32 = jnp.int32


def substep_powers():
    one = np.array([1.0 / np.prod(np.arange(1, k + 1)) for k in range(TERMS + 1)])
    total = np.array([1.0])
    for _ in range(SUBSTEPS):
        total = np.convolve(total, one)
    return [float(c) for c in total]


COEF = substep_powers()
DEG = SUBSTEPS * TERMS
HALF = DEG // 2


def hi_lo(x):
    hi = x.astype(BF16)
    return hi, (x - hi.astype(F32)).astype(BF16)


def right3(x):
    hi, lo = hi_lo(x)
    return jnp.concatenate([hi, hi, lo], axis=0)


def left3(m):
    hi, lo = hi_lo(m)
    return jnp.concatenate([hi, lo, hi], axis=1)


def dot(a, b):
    return jnp.dot(a, b, preferred_element_type=F32)


def one_hot(row, base):
    n = row.shape[1]
    line = lax.broadcasted_iota(I32, (KB, n), 0).astype(F32).astype(BF16)
    row = jnp.minimum(jnp.maximum(row - base, -1), KB).astype(F32).astype(BF16)
    return jnp.where(line == jnp.broadcast_to(row, (KB, n)), jnp.bfloat16(1), jnp.bfloat16(0))


def look_up(table, index):
    lane = index & 127
    tile = index >> 7
    out = jnp.zeros(index.shape, table.dtype)
    for m in range(table.shape[1] // 128):
        part = jnp.broadcast_to(table[:, 128 * m : 128 * m + 128], index.shape)
        got = jnp.take_along_axis(part, lane, axis=1, mode="promise_in_bounds")
        out = jnp.where(tile == m, got, out)
    return out


def kernel(
    secs,
    rads,
    fields_hbm,
    pattern_hbm,
    order_hbm,
    sizes_hbm,
    neighbours_hbm,
    sends_hbm,
    operator_hbm,
    trace_hbm,
    lift_hbm,
    heights_hbm,
    out,
    fields,
    pattern,
    order,
    sizes,
    neighbours,
    sends,
    operator,
    trace_map,
    lift_map,
    tent_height,
    in_sem,
    tp,
    ap,
    lp,
    t3,
    a3,
    l3,
    rows,
    erow,
    ehi,
    elo,
    scatter,
    ends,
    sofar,
    pick,
    listed,
    catch,
    nbx,
    height,
    flow,
    fresh,
    part,
    gath,
    loaded,
    sb,
    rb,
    send_sem,
    recv_sem,
):
    s = lax.axis_index("sector")
    r = lax.axis_index("radial")
    up = lax.rem(s + 1, secs)
    down = lax.rem(s + secs - 1, secs)

    loads = {
        name: pltpu.make_async_copy(src, dst, in_sem.at[i])
        for i, (name, src, dst) in enumerate(
            [
                ("sends", sends_hbm, sends),
                ("trace", trace_hbm, trace_map),
                ("fields", fields_hbm, fields),
                ("operator", operator_hbm, operator),
                ("order", order_hbm, order),
                ("sizes", sizes_hbm, sizes),
                ("neighbours", neighbours_hbm, neighbours),
                ("pattern", pattern_hbm, pattern),
                ("heights", heights_hbm, tent_height),
                ("lift", lift_hbm, lift_map),
            ]
        )
    }
    urgent = ("fields", "sends", "trace")
    for name in urgent:
        loads[name].start()

    rb[:, :, TRACE:TP] = jnp.zeros((LEVELS, 4, TP - TRACE, BND), F32)

    @pl.when(r == 0)
    def _():
        rb[:, 2] = jnp.zeros((LEVELS, TP, BND), F32)

    @pl.when(r == rads - 1)
    def _():
        rb[:, 3] = jnp.zeros((LEVELS, TP, BND), F32)

    barrier = pltpu.get_barrier_semaphore()

    def greet(a, b):
        pl.semaphore_signal(barrier, inc=1, device_id=(a, b), device_id_type=MESH)

    greet(up, r)
    greet(down, r)

    @pl.when(r > 0)
    def _():
        greet(s, r - 1)

    @pl.when(r < rads - 1)
    def _():
        greet(s, r + 1)

    for name in loads:
        if name not in urgent:
            loads[name].start()

    def copy(level, group, a, b):
        return pltpu.make_async_remote_copy(
            src_ref=sb.at[level, group, pl.ds(0, TRACE)],
            dst_ref=rb.at[level, group, pl.ds(0, TRACE)],
            send_sem=send_sem.at[level % 2, group],
            recv_sem=recv_sem.at[level % 2, group],
            device_id=(a, b),
            device_id_type=MESH,
        )

    def start(level):
        @pl.when(r < rads - 1)
        def _():
            copy(level, 2, s, r + 1).start()

        @pl.when(r > 0)
        def _():
            copy(level, 3, s, r - 1).start()

        copy(level, 0, up, r).start()
        copy(level, 1, down, r).start()

    def arrive(level):
        copy(level, 0, up, r).wait_recv()
        copy(level, 1, down, r).wait_recv()

        @pl.when(r > 0)
        def _():
            copy(level, 2, s, r - 1).wait_recv()

        @pl.when(r < rads - 1)
        def _():
            copy(level, 3, s, r + 1).wait_recv()

    def drain(level):
        copy(level, 0, up, r).wait_send()
        copy(level, 1, down, r).wait_send()

        @pl.when(r < rads - 1)
        def _():
            copy(level, 2, s, r + 1).wait_send()

        @pl.when(r > 0)
        def _():
            copy(level, 3, s, r - 1).wait_send()

    def fill_sends(level, got):
        for d in range(4):
            piece = got[:, BND * d : BND * d + BND]
            sb[level, d] = piece[:TP] + piece[TP:]

    tp[...] = jnp.zeros((TP, CP), F32)
    loads["sends"].wait()
    for m in range(ELEMS // KB):
        listed[KB * m : KB * m + KB] = one_hot(sends[...], KB * m)
    loads["trace"].wait()
    tp[0:TRACE, 0:COMP] = trace_map[...]
    t3[0:TP] = left3(tp[...])
    loads["fields"].wait()
    piece = [fields[pl.ds(t, COMP, stride=TILES)] for t in range(TILES)]
    piece = jnp.concatenate(piece, axis=1)
    piece = jnp.concatenate([piece, jnp.zeros((CP - COMP, ELEMS), F32)], axis=0)
    hi, lo = hi_lo(piece)
    o = dot(t3[0:TP], jnp.concatenate([hi, hi, lo], axis=0))
    o = jnp.concatenate(hi_lo(o), axis=0)
    got = dot(o, listed[...])
    fill_sends(0, got)
    pl.semaphore_wait(
        barrier, 2 + jnp.where(r > 0, 1, 0) + jnp.where(r < rads - 1, 1, 0)
    )
    start(0)
    flow[...] = o
    rows[0:CP] = hi
    rows[CP : 2 * CP] = lo

    ap[...] = jnp.zeros((CP, CP), F32)
    lp[...] = jnp.zeros((FACES * TP, 256), F32)
    loads["operator"].wait()
    ap[0:COMP, 0:COMP] = operator[...]
    p1 = ap[...]
    a3[0:CP] = left3(p1)
    b1 = right3(p1)
    p2 = dot(a3[0:CP], b1)
    a3[CP : 2 * CP] = left3(p2)
    b2 = right3(p2)
    p34 = dot(a3[0 : 2 * CP], b2)
    a3[2 * CP : 4 * CP] = left3(p34)
    b4 = right3(p34[CP:])
    t3[TP : 2 * TP] = left3(dot(t3[0:TP], b1))
    t3[2 * TP : 4 * TP] = left3(dot(t3[0 : 2 * TP], b2))
    t3[4 * TP : 8 * TP] = left3(dot(t3[0 : 4 * TP], b4))
    t3[8 * TP : 9 * TP] = left3(dot(t3[4 * TP : 5 * TP], b4))

    for name in ("order", "sizes", "neighbours", "pattern", "heights"):
        loads[name].wait()
    line = lax.broadcasted_iota(I32, (16, 128), 0)
    lane = lax.broadcasted_iota(I32, (16, 128), 1)
    shift = jnp.zeros((16, 128), I32)
    limit = jnp.zeros((16, 128), I32)
    begin = jnp.int32(0)
    for l in range(LEVELS):
        size = sizes[l]
        mine = (line >= 3 * l) & (line < 3 * l + 3)
        shift = jnp.where(mine, begin - BLOCK * l, shift)
        limit = jnp.where(mine, BLOCK * l + size, limit)
        begin = begin + size
    slot = 128 * line + lane
    place = jnp.minimum(jnp.maximum(slot + shift, 0), ELEMS - 1)
    element = jnp.where(slot < limit, look_up(order[...], place), -1)
    tall = jnp.concatenate([element >> 7, element & 127, jnp.zeros((96, 128), I32)], axis=0).astype(F32)
    tall = jnp.transpose(tall)
    for l in range(LEVELS):
        for t in range(3):
            n = 3 * l + t
            erow[l, :, 128 * t : 128 * t + 128] = element[n : n + 1]
            here = slice(128 * t, 128 * t + 128)
            ehi[l, here] = jnp.broadcast_to(tall[:, n : n + 1], (128, 128)).astype(BF16)
            elo[l, here] = jnp.broadcast_to(tall[:, n + 16 : n + 17], (128, 128)).astype(BF16)
    line = lax.broadcasted_iota(I32, (8, ELEMS), 0)
    extra = jnp.where(line == 0, jnp.broadcast_to(pattern[...], (8, ELEMS)), 0)
    near = neighbours[...]
    numbers = jnp.concatenate([near >> 8, near & 255, extra], axis=0)
    rows[2 * CP :] = numbers.astype(F32).astype(BF16)
    loads["lift"].wait()
    for f in range(FACES):
        lp[TP * f : TP * f + TRACE, 0:COMP] = lift_map[:, f]
    l3[...] = left3(jnp.transpose(lp[...])[0:CP])

    def powers(l):
        h = height[l]
        ps = [jnp.ones_like(h)]
        for k in range(DEG):
            ps.append(ps[k] * h)
        return ps

    def by_face(got):
        his = [got[:TP, BLOCK * f : BLOCK * f + BLOCK] for f in range(FACES)]
        los = [got[TP:, BLOCK * f : BLOCK * f + BLOCK] for f in range(FACES)]
        return jnp.concatenate(his + his + los, axis=0)

    def traces(os, hs):
        o = os[0:TP]
        for k in range(1, DEG + 1):
            o += os[TP * k : TP * k + TP] * (hs[k] * COEF[k])
        return o

    def finish(l):
        x = loaded[...]
        x3 = right3(x)
        hs = powers(l)
        y, v = x, x * COEF[HALF]
        for k in range(1, HALF + 1):
            u = dot(a3[CP * (k - 1) : CP * k], x3)
            if k < HALF:
                y += u * (hs[k] * COEF[k])
            v += u * (hs[k] * COEF[HALF + k])
        y += dot(a3[CP * (HALF - 1) :], right3(v * hs[HALF]))
        ends[:, BLOCK * l : BLOCK * l + BLOCK] = jnp.concatenate(hi_lo(y), axis=0)

    def put(first, last, add):
        here = slice(BLOCK * first, BLOCK * last)
        for n in range(ELEMS // KB):
            got = dot(ends[:, here], scatter[here, KB * n : KB * n + KB])
            got = got[:CP] + got[CP:]
            if not add:
                sofar[:, KB * n : KB * n + KB] = got
                continue
            got = (sofar[:, KB * n : KB * n + KB] + got)[:COMP]
            for t in range(KB // 128):
                place = pl.ds(n * (KB // 128) + t, COMP, stride=TILES)
                out[place] = got[:, 128 * t : 128 * t + 128]

    for l in range(LEVELS):
        if l > 0:
            finish(l - 1)
            ones = jnp.ones((16, BLOCK), BF16)
            for n in range(ELEMS // KB):
                here = slice(KB * n, KB * n + KB)
                back = scatter[BLOCK * (l - 1) : BLOCK * l, here]
                got = dot(jnp.concatenate([fresh[...], ones], axis=0), back)
                keep = jnp.broadcast_to(1.0 - got[2 * TP : 2 * TP + 1], (2 * TP, KB))
                flow[:, here] = (flow[:, here].astype(F32) * keep + got[: 2 * TP]).astype(BF16)

        moved = jnp.zeros((2 * CP + 16, BLOCK), F32)
        for m in range(ELEMS // KB):
            moved += dot(rows[:, KB * m : KB * m + KB], one_hot(erow[l], KB * m))
        loaded[...] = moved[:CP] + moved[CP : 2 * CP]
        numbers = moved[2 * CP :].astype(I32)
        near = numbers[0:4] * 256 + numbers[4:8]
        for f in range(FACES):
            nbx[:, BLOCK * f : BLOCK * f + BLOCK] = near[f : f + 1]
        kind = numbers[8:9]
        h = jnp.zeros((1, BLOCK), F32)
        for p in range(16):
            h = jnp.where(kind == p, tent_height[p], h)
        height[l] = h
        for f in range(0, FACES * BLOCK, 2 * KB):
            here = slice(f, f + 2 * KB)
            row = nbx[:, here]
            acc = jnp.zeros((2 * TP, 2 * KB), F32)
            for m in range(ELEMS // KB):
                acc += dot(flow[:, KB * m : KB * m + KB], one_hot(row, KB * m))
            gath[:, here] = acc.astype(BF16)
            for m in range(SLOTS // KB):
                catch[KB * m : KB * m + KB, here] = one_hot(row, ELEMS + KB * m)
        loaded[...] += dot(l3[...], by_face(gath[...]))
        one, none = jnp.bfloat16(1), jnp.bfloat16(0)
        lane = lax.broadcasted_iota(I32, (BLOCK, 128), 1).astype(F32).astype(BF16)
        same = jnp.where(elo[l] == lane, one, none)
        for t in range(TILES):
            hit = jnp.where(ehi[l] == jnp.bfloat16(t), same, none)
            scatter[BLOCK * l : BLOCK * l + BLOCK, 128 * t : 128 * t + 128] = hit
        if l < LEVELS - 1:
            got = dot(flow[...], listed[...])
            for d in range(4):
                row = sends[:, BND * d : BND * d + BND]
                row = [
                    jnp.broadcast_to(digit.astype(F32).astype(BF16), (BLOCK, BND))
                    for digit in (row >> 7, row & 127)
                ]
                hit = jnp.where(elo[l] == row[1], one, none)
                pick[:, BND * d : BND * d + BND] = jnp.where(ehi[l] == row[0], hit, none)
            gone = dot(jnp.ones((16, BLOCK), BF16), pick[...])[0:1]
            part[...] = got * jnp.broadcast_to(1.0 - gone, (2 * TP, SLOTS))
        if l == LEVELS - 1:
            put(0, l, False)
        drain(l)
        arrive(l)
        got = jnp.concatenate([rb[l, d] for d in range(4)], axis=1)
        got = dot(jnp.concatenate(hi_lo(got), axis=0), catch[...]).astype(BF16)
        x = loaded[...] + dot(l3[...], by_face(got))
        loaded[...] = x
        if l < LEVELS - 1:
            o = traces(dot(t3[...], right3(x)), powers(l))
            o = jnp.concatenate(hi_lo(o), axis=0)
            fresh[...] = o
            fill_sends(l + 1, part[...] + dot(o, pick[...]))
            start(l + 1)

    finish(LEVELS - 1)
    put(LEVELS - 1, LEVELS, True)

def solution(mesh):
    secs, rads = mesh.shape["sector"], mesh.shape["radial"]
    hbm = pl.BlockSpec(memory_space=pltpu.HBM)

    def body(
        fields,
        pattern,
        tent_order,
        level_sizes,
        send_rows,
        neighbours,
        operator,
        trace_map,
        lift_map,
        tent_height,
    ):
        args = (
            fields.reshape(COMP * TILES, 128),
            pattern[0],
            tent_order[0],
            level_sizes[0, 0],
            neighbours[0, 0],
            send_rows.reshape(1, SLOTS),
            operator,
            trace_map,
            jnp.transpose(lift_map, (2, 0, 1)),
            tent_height,
        )
        args = tuple(pltpu.with_memory_space_constraint(a, pltpu.HBM) for a in args)
        homes = [
            (pltpu.SMEM if len(a.shape) == 1 else pltpu.VMEM)(a.shape, a.dtype) for a in args
        ]
        out = pl.pallas_call(
            functools.partial(kernel, secs, rads),
            out_shape=jax.ShapeDtypeStruct((COMP * 8, 128), F32),
            in_specs=[hbm] * len(args),
            out_specs=pl.BlockSpec(memory_space=pltpu.VMEM),
            scratch_shapes=homes
            + [
                pltpu.SemaphoreType.DMA((len(args),)),
                pltpu.VMEM((TP, CP), F32),
                pltpu.VMEM((CP, CP), F32),
                pltpu.VMEM((FACES * TP, 256), F32),
                pltpu.VMEM(((DEG + 1) * TP, 3 * CP), BF16),
                pltpu.VMEM((HALF * CP, 3 * CP), BF16),
                pltpu.VMEM((CP, 3 * FACES * TP), BF16),
                pltpu.VMEM((2 * CP + 16, ELEMS), BF16),
                pltpu.VMEM((LEVELS, 1, BLOCK), I32),
                pltpu.VMEM((LEVELS, BLOCK, 128), BF16),
                pltpu.VMEM((LEVELS, BLOCK, 128), BF16),
                pltpu.VMEM((LEVELS * BLOCK, ELEMS), BF16),
                pltpu.VMEM((2 * CP, LEVELS * BLOCK), BF16),
                pltpu.VMEM((CP, ELEMS), F32),
                pltpu.VMEM((BLOCK, SLOTS), BF16),
                pltpu.VMEM((ELEMS, SLOTS), BF16),
                pltpu.VMEM((SLOTS, FACES * BLOCK), BF16),
                pltpu.VMEM((1, FACES * BLOCK), I32),
                pltpu.VMEM((LEVELS, 1, BLOCK), F32),
                pltpu.VMEM((2 * TP, ELEMS), BF16),
                pltpu.VMEM((2 * TP, BLOCK), BF16),
                pltpu.VMEM((2 * TP, SLOTS), F32),
                pltpu.VMEM((2 * TP, FACES * BLOCK), BF16),
                pltpu.VMEM((CP, BLOCK), F32),
                pltpu.VMEM((LEVELS, 4, TP, BND), F32),
                pltpu.VMEM((LEVELS, 4, TP, BND), F32),
                pltpu.SemaphoreType.DMA((2, 4)),
                pltpu.SemaphoreType.DMA((2, 4)),
            ],
            compiler_params=pltpu.CompilerParams(
                collective_id=0, has_side_effects=True, vmem_limit_bytes=32 * 2**20
            ),
            name="tent_layer",
        )(*args)
        return out.reshape(1, 1, COMP, ELEMS)

    block = P("sector", "radial", None)
    wide = P("sector", "radial", None, None)
    return jax.shard_map(
        body,
        mesh=mesh,
        in_specs=(wide, block, block, block, wide, wide, P(), P(), P(), P()),
        out_specs=wide,
        check_vma=False,
    )
```
